32 devices in a mesh: view: 4 (over x, core), gy: 2 (over y), gz: 4 (over z).
Axes of the slice: x: 2, y: 2, z: 4, core: 2. Of those that a mesh axis runs over, the one named last changes fastest.
Arguments:
- estimate: float32 [16, 128, 1024], P('view', 'gy', 'gz'), may hold values from 0.5 to 2
- view_data: bfloat16 [8, 16, 128, 1024], P('view', None, 'gy', 'gz'), may hold values from 0.25 to 2
- block_scales: float32 [8, 4, 16], P('view', 'gy', 'gz'), may hold values from 0.5 to 2
- block_flags: int32 [8, 4, 16], P('view', 'gy', 'gz'), may hold values 0 or 1
- profile: float32 [8, 3, 33], P('view'), may hold values from 0.05 to 1
- supports: int32 [8, 3], P('view'), may hold values from 1 to 16, as said below
Outputs:
- refined: float32 [16, 128, 1024], P('view', 'gy', 'gz')
The draws below stay inside these ranges and needn't reach their ends.
Inputs may be any that keep to these rules, and one draw needn't show every extreme that they name: supports[v] holds view v's half-widths along x, y and z: along x 1 to 6, along y and z 1 to 16; some view has 6 along x, some view 16 along y and some view 16 along z. block_flags[v, b, c] is 1 where view v's data in the block of 32 x 64 cells (b, c) are valid.
All inputs are finite; a program needn't handle non-finite values.
Results may differ from the reference program's by a relative error of at most 0.0003.
Values sent between devices are 32-bit elements; how exact they have to be, the bound alone decides.
A program may use at most 64 MiB of HBM per device.

```python
import math
import jax
import jax.numpy as jnp
from jax import lax

R = 16
RX = 6
NX = 16
BY = 32
BZ = 64
ITERS = 2
VIEWS = 8
NY = 128
NZ = 1024


def draw_supports(key, part):
    key_list = jax.random.split(jax.random.fold_in(key, 11), 3)
    along_planes = jax.random.randint(key_list[0], (VIEWS, 1), 1, RX + 1)
    along_cells = jax.random.randint(key_list[1], (VIEWS, 2), 1, R + 1)
    chosen = jax.random.randint(key_list[2], (3,), 0, VIEWS)
    row_index = jnp.arange(VIEWS)[:, None]
    col_index = jnp.arange(2)[None, :]
    along_planes = jnp.where(row_index == chosen[0], RX, along_planes)
    along_cells = jnp.where((row_index == chosen[1]) & (col_index == 0), R, along_cells)
    along_cells = jnp.where((row_index == chosen[2]) & (col_index == 1), R, along_cells)
    return jnp.concatenate([along_planes, along_cells], axis=1).astype(jnp.int32)


def set_ends(array, rng, least, high):
    dims = array.shape
    place = [jax.random.randint(jax.random.fold_in(rng, axis), (), 0, dims[axis]) for axis in range(len(dims))]
    array = array.at[tuple(place)].set(least)
    longest = dims.index(max(dims))
    place[longest] = (place[longest] + 1) % dims[longest]
    return array.at[tuple(place)].set(high)


def levels(own_key, shape, pieces, least, top_value):
    level, own = 1.0, jax.random.fold_in(own_key, 6)
    for axis_at, parts in pieces:
        steps = jnp.exp(jax.random.uniform(jax.random.fold_in(own, axis_at), (parts,), jnp.float32, least / len(pieces), top_value / len(pieces)))
        level = level * jnp.repeat(steps, shape[axis_at] // parts).reshape([-1 if axis == axis_at else 1 for axis in range(len(shape))])
    return level


def setup_inputs(seed: int = 0) -> dict:
    seeds = jax.random.split(jax.random.key(seed), 7)
    estimate = jnp.clip(0.5 + 1.5 * jax.random.uniform(seeds[0], (NX, NY, NZ), jnp.float32) ** levels(seeds[0], (NX, NY, NZ), ((0, 4), (1, 2), (2, 4)), -0.2, 0.2), 0.5, 2.0)
    view_data = jnp.clip(0.25 + 1.75 * jax.random.uniform(seeds[1], (VIEWS, NX, NY, NZ), jnp.float32) ** levels(seeds[1], (VIEWS, NX, NY, NZ), ((0, 4), (2, 2), (3, 4)), -0.2, 0.2), 0.25, 2.0).astype(jnp.bfloat16)
    block_scales = jnp.clip(jnp.exp(math.log(2.0) - 1.3862944 * jax.random.uniform(seeds[2], (VIEWS, NY // BY, NZ // BZ), jnp.float32) ** levels(seeds[2], (VIEWS, NY // BY, NZ // BZ), ((0, 4), (1, 2), (2, 4)), -0.2, 0.2)), 0.5, 2.0)
    block_flags = set_ends((jax.random.randint(seeds[3], (VIEWS, NY // BY, NZ // BZ), 0, 4) < 3).astype(jnp.int32), jax.random.fold_in(seeds[3], 1), 0, 1)
    profile = jnp.clip(jnp.exp(math.log(1.0) - 2.9957323 * jax.random.uniform(seeds[4], (VIEWS, 3, 2 * R + 1), jnp.float32) ** levels(seeds[4], (VIEWS, 3, 2 * R + 1), ((0, 4),), -0.2, 0.2)), 0.05, 1.0)
    supports = draw_supports(jax.random.fold_in(seeds[6], 71), 0)
    return {"estimate": estimate, "view_data": view_data, "block_scales": block_scales, "block_flags": block_flags, "profile": profile, "supports": supports}


def band_matrix(tap_table, row_count, col_count, offset):
    row_index = lax.broadcasted_iota(jnp.int32, (row_count, col_count), 0)
    col_index = lax.broadcasted_iota(jnp.int32, (row_count, col_count), 1)
    lag_index = row_index - col_index + offset

    def place_tap(tap_index, summed):
        return jnp.where(lag_index == tap_index, tap_table[tap_index], summed)

    return lax.fori_loop(0, tap_table.shape[0], place_tap, jnp.zeros((row_count, col_count), jnp.float32))


def kernel_table(profile, supports):
    tap_count = profile.shape[-1]
    distance = jnp.abs(jnp.arange(tap_count, dtype=jnp.int32) - (tap_count - 1) // 2)
    inside = distance[None, None, :] <= supports[:, :, None]
    masked = jnp.where(inside, profile, 0.0)
    return masked / jnp.sum(masked, axis=-1, keepdims=True)


def blur_axis(field, kernel, axis):
    half_width = (kernel.shape[0] - 1) // 2
    tile_size = 2 * half_width
    rotated = jnp.moveaxis(field, axis, -1)
    length = rotated.shape[-1]
    padded = jnp.pad(rotated, [(0, 0)] * (rotated.ndim - 1) + [(half_width, half_width)])
    blocks = padded.reshape(rotated.shape[:-1] + (length // tile_size + 1, tile_size))
    band_full = band_matrix(kernel, 2 * tile_size, tile_size, 0)
    leading = jnp.einsum('...bj,ji->...bi', blocks[..., :-1, :], band_full[:tile_size], precision=lax.Precision.HIGHEST)
    second = jnp.einsum('...bj,ji->...bi', blocks[..., 1:, :], band_full[tile_size:], precision=lax.Precision.HIGHEST)
    return jnp.moveaxis((leading + second).reshape(rotated.shape), -1, axis)


def blur(field, kernel_rows):
    half_width = (kernel_rows.shape[1] - 1) // 2
    planes = field.shape[0]
    plane_band = band_matrix(kernel_rows[0], planes, planes, half_width)
    mixed_planes = jnp.einsum('jyz,ji->iyz', field, plane_band, precision=lax.Precision.HIGHEST)
    along_rows = blur_axis(mixed_planes, kernel_rows[1], 1)
    return blur_axis(along_rows, kernel_rows[2], 2)


def reference(estimate, view_data, block_scales, block_flags, profile, supports):
    forward = kernel_table(profile, supports)
    backward = forward[:, :, ::-1]
    view_count = view_data.shape[0]
    current = estimate
    for iteration in range(ITERS):
        def add_view(view_index, totals):
            blurred = blur(current, forward[view_index])
            scale_map = jnp.repeat(jnp.repeat(block_scales[view_index], BY, axis=0), BZ, axis=1)
            valid_map = jnp.repeat(jnp.repeat(block_flags[view_index], BY, axis=0), BZ, axis=1)
            measured = view_data[view_index].astype(jnp.float32) * scale_map[None]
            ratios = jnp.where(valid_map[None] == 1, measured / blurred, 1.0)
            return totals + blur(ratios, backward[view_index])

        corrections = lax.fori_loop(0, view_count, add_view, jnp.zeros(current.shape, jnp.float32))
        current = current * corrections / view_count
    return current
```

```python
import contextlib
import functools

import jax
import jax.numpy as jnp
from jax import lax
from jax.experimental import pallas as pl
from jax.experimental.pallas import tpu as pltpu
from jax.sharding import PartitionSpec as P

BY = 32
BZ = 64
ITERS = 2
LANES = 128
MESH = pl.DeviceIdType.MESH
BF = jnp.bfloat16
F32 = jnp.float32


def scope(name):
    return contextlib.nullcontext()


def lane_iota(rows):
    return lax.broadcasted_iota(jnp.int32, (rows, LANES), 1)


def toeplitz(row, rows, shift):
    wide = jnp.broadcast_to(row, (rows, LANES))
    return pltpu.roll(wide, shift % LANES, 1, stride=1, stride_axis=0)


def roll_lanes(x, shift):
    shift = shift % LANES
    return pltpu.roll(x, shift, x.ndim - 1) if shift else x


def build_taps(dst, profile, supports, views):
    taps = profile.shape[2]
    dst[...] = jnp.zeros_like(dst)
    for vv in range(views):
        for a in range(3):
            r = 3 * vv + a
            dst[0, r : r + 1, :taps] = profile[a, vv : vv + 1, :]
    rows = dst.shape[1]
    row = lax.broadcasted_iota(jnp.int32, (rows, LANES), 0)
    lane = lane_iota(rows)
    reach = jnp.zeros((rows, LANES), jnp.int32)
    for vv in range(views):
        for a in range(3):
            reach = jnp.where(row == 3 * vv + a, supports[vv, a], reach)
    inside = (jnp.abs(lane - (taps - 1) // 2) <= reach) & (row < 3 * views)
    masked = jnp.where(inside, dst[0], 0.0)
    total = jnp.sum(masked, axis=1, keepdims=True)
    table = masked / jnp.where(total > 0.0, total, 1.0)
    turn = lax.broadcasted_iota(jnp.int32, (LANES, LANES), 0) + lax.broadcasted_iota(
        jnp.int32, (LANES, LANES), 1
    )
    flip = (turn == taps - 1).astype(F32)
    dst[0] = table
    dst[1] = jnp.dot(table, flip, precision=lax.Precision.HIGHEST, preferred_element_type=F32)


def build_plane_row(dst, row_base, kx, ky, planes, hw):
    lane = lane_iota(hw)
    per_tile = LANES // hw
    halves = planes // per_tile
    tall = toeplitz(ky, hw, 0)
    bands = []
    for d in range(3):
        q = jnp.where(lane < hw, roll_lanes(tall, -hw * d), 0.0)
        width = hw
        while width < LANES:
            q = q + roll_lanes(q, width)
            width *= 2
        bands.append(q)
    tx = toeplitz(kx, planes, -hw)
    row_id = lax.broadcasted_iota(jnp.int32, (LANES, LANES), 0)
    group = lax.broadcasted_iota(jnp.int32, (LANES, LANES), 1) // hw
    for half in range(halves):
        pick = (row_id == group + half * per_tile).astype(F32)
        spread = jnp.dot(tx, pick, precision=lax.Precision.HIGHEST, preferred_element_type=F32)
        for d in range(3):
            for x in range(planes):
                tile = spread[x : x + 1, :] * bands[d]
                c0 = (halves * d + half) * LANES
                dst[row_base + x * hw : row_base + (x + 1) * hw, c0 : c0 + LANES] = tile.astype(BF)


def build_depth(dst, v, kz, rows_z, hw):
    row_j = lax.broadcasted_iota(jnp.int32, (rows_z, LANES), 0)
    lane = lane_iota(rows_z)
    reps = rows_z // LANES
    t = jnp.concatenate([toeplitz(kz, LANES, -hw)] * reps, axis=0)
    for ct in range(reps):
        c = lane + ct * LANES
        keep = jnp.abs(c - row_j) <= hw
        dst[v, :, ct * LANES : (ct + 1) * LANES] = jnp.where(keep, t, 0.0).astype(BF)
    h = jnp.concatenate([toeplitz(kz, LANES, 0)] * reps, axis=0)
    low = (row_j < hw) & (lane < hw)
    high = (row_j >= rows_z - hw) & (lane >= hw) & (lane < 2 * hw)
    h = jnp.where(low, h, 0.0) + roll_lanes(jnp.where(high, h, 0.0), LANES // 2 - hw)
    width = hw
    while width < LANES // 2:
        h = h + roll_lanes(h, width)
        width *= 2
    dst[v, :, rows_z : rows_z + LANES] = h.astype(BF)


def sem_bases(ne):
    names = [
        ("x", ne), ("core", 2 * ne), ("yu", 2), ("yd", 2), ("z", 4 * ne), ("r1", 2 * ne),
        ("r1z", 2), ("zb", 6), ("yb", 4), ("r2", 2 * ne), ("zx", 2),
    ]
    bases, count = {}, 0
    for name, size in names:
        bases[name] = count
        count += size
    return bases, count


def kernel(
    sizes, est, vd_any, scales_any, flags_any, profile_any, supports_any, out,
    scales, flags, profile, supports, taps,
    fg, fb, am, bm, mt, gp, gh, ob, r1, tt, r2, yi, et, wk, wi, pk, zp, r1z, zo, zi, zt, zx, zr, vd,
    lsem, ssem, rsem,
):
    ny, nz, views, planes, rows_y, rows_z, own, hw = sizes
    nb = rows_y // hw
    ne = nb + 2
    blk = planes * hw
    half = LANES // 2
    v = lax.axis_index("view")
    gy = lax.axis_index("gy")
    gz = lax.axis_index("gz")
    va, vb, vc = (lax.bitwise_xor(v, 1), lax.bitwise_xor(v, 2), lax.bitwise_xor(v, 3))
    has_up, has_dn = (gy > 0, gy < ny - 1)
    has_lf, has_rt = (gz > 0, gz < nz - 1)
    yup, ydn = (jnp.maximum(gy - 1, 0), jnp.minimum(gy + 1, ny - 1))
    zlf, zrt = (jnp.maximum(gz - 1, 0), jnp.minimum(gz + 1, nz - 1))
    to_a, to_b = ({"view": va}, {"view": vb})
    to_up, to_dn = ({"gy": yup}, {"gy": ydn})
    to_lf, to_rt = ({"gz": zlf}, {"gz": zrt})
    z_dev = [[to_lf, {"gz": zlf, "view": va}], [to_rt, {"gz": zrt, "view": va}]]
    z_has = [has_lf, has_rt]
    y_has = [has_up, has_dn]
    y_to = [to_up, to_dn]
    y_co = [yup, ydn]
    z_co = [zlf, zrt]
    view_total = views * 4
    pair = (v, vb)
    other = (va, vc)
    sid, _ = sem_bases(ne)

    def mine(o):
        return pl.ds(o * own, own)

    def rcopy(src, dst, it, s, dev):
        return pltpu.make_async_remote_copy(
            src_ref=src, dst_ref=dst, send_sem=ssem.at[it, s], recv_sem=rsem.at[it, s],
            device_id=dev, device_id_type=MESH,
        )

    def landed(dst, it, s, dev):
        rcopy(dst, dst, it, s, dev).wait_recv()

    def sent(src, it, s, dev):
        rcopy(src, src, it, s, dev).wait_send()

    def flipped(e):
        return jnp.where(has_dn, e, nb + 1 - e)

    def used(e):
        return ((e > 0) | has_up) & ((e < nb + 1) | has_dn)

    est_load = [
        pltpu.make_async_copy(
            est.at[:, b * hw : (b + 1) * hw, :], fg.at[0, b + 1, mine(v)], lsem.at[5 + b]
        )
        for b in range(nb)
    ]
    small = [
        pltpu.make_async_copy(s, d, lsem.at[i])
        for i, (s, d) in enumerate((
            (profile_any, profile), (supports_any, supports), (scales_any, scales), (flags_any, flags),
        ))
    ]
    load = pltpu.make_async_copy(vd_any, vd, lsem.at[4])
    for c in est_load:
        c.start()
    for c in small:
        c.start()
    load.start()

    barrier = pltpu.get_barrier_semaphore()
    meets = [(None, to_a), (None, to_b), (has_up, to_up), (has_dn, to_dn)]
    for d in range(2):
        for c in range(2):
            meets.append((z_has[d], z_dev[d][c]))
            for u in range(2):
                dev = dict(z_dev[d][c], gy=y_co[u])
                meets.append((z_has[d] & y_has[u], dev))
    expected = jnp.int32(0)
    for cond, dev in meets:
        if cond is None:
            pl.semaphore_signal(barrier, inc=1, device_id=dev, device_id_type=MESH)
            expected = expected + 1
        else:
            @pl.when(cond)
            def _():
                pl.semaphore_signal(barrier, inc=1, device_id=dev, device_id_type=MESH)
            expected = expected + cond.astype(jnp.int32)

    for d in range(2):
        @pl.when(jnp.logical_not(z_has[d]))
        def _():
            for it in range(ITERS):
                for c in range(2):
                    wi[it, d, c] = jnp.zeros((ne, hw, LANES), F32)
                zi[it, d] = jnp.zeros((ne, hw, LANES), F32)

        for u, e in ((0, 0), (1, nb + 1)):
            @pl.when(z_has[d] & jnp.logical_not(y_has[u]))
            def _():
                for it in range(ITERS):
                    zi[it, d, e] = jnp.zeros((hw, LANES), F32)

    with scope('barrier'):
      for c in est_load:
        c.wait()
      pl.semaphore_wait(barrier, expected)

    def core_send(it, e, k):
        ref = fg.at[it, e, mine(pair[k])]
        rcopy(ref, ref, it, sid["core"] + 2 * e + k, to_a).start()

    def y_send(it, e, ks):
        for u, e_from, e_to, name in ((0, 1, nb + 1, "yu"), (1, nb, 0, "yd")):
            @pl.when(y_has[u] & (e == e_from))
            def _():
                for k in ks:
                    rcopy(
                        fg.at[it, e_from, mine(pair[k])], fg.at[it, e_to, mine(pair[k])],
                        it, sid[name] + k, y_to[u],
                    ).start()

    def x_send(e):
        ref = fg.at[0, e, mine(v)]
        rcopy(ref, ref, 0, sid["x"] + e, to_b).start()

    lane_h = lane_iota(hw)
    group_h = lane_h // hw
    main = slice(1, nb + 1)

    def edges(it, e, k):
        tile = jnp.zeros((hw, LANES), F32)
        for p in range(own):
            body = fg[it, e, own * pair[k] + p]
            tile = jnp.where(group_h == p, roll_lanes(body[:, :LANES], hw * p), tile)
            tile = jnp.where(
                group_h == own + p, roll_lanes(body[:, rows_z - LANES :], hw * (own + p + 1)), tile
            )
        et[it, k, e] = tile

    def by_side(near, far):
        return (
            jnp.where(lane_h < half, near, roll_lanes(far, half)),
            jnp.where(lane_h < half, roll_lanes(near, half), far),
        )

    def z_sid(side, c, e):
        return sid["z"] + (2 * side + c) * ne + e

    def z_send(it, e):
        for d in range(2):
            for c in range(2):
                @pl.when(z_has[d])
                def _():
                    rcopy(wk.at[it, d, e], wi.at[it, 1 - d, c, e], it, z_sid(1 - d, c, e), z_dev[d][c]).start()

    def diag_send(it, e):
        for u, e_from, e_to in ((0, 1, nb + 1), (1, nb, 0)):
            for d in range(2):
                @pl.when(z_has[d] & y_has[u] & (e == e_from))
                def _():
                    for c in range(2):
                        rcopy(
                            wk.at[it, d, e_from], wi.at[it, 1 - d, c, e_to], it,
                            z_sid(1 - d, c, e_to), dict(z_dev[d][c], gy=y_co[u]),
                        ).start()

    def z_split(it, e):
        wk[it, 0, e], wk[it, 1, e] = by_side(et[it, 0, e], et[it, 1, e])

    def gather(it, e):
        for k in range(2):
            landed(fg.at[it, e, mine(other[k])], it, sid["core"] + 2 * e + k, to_a)
        fb[pl.ds(pl.multiple_of(e * blk, blk), blk), :rows_z] = fg[it, e].reshape(blk, rows_z).astype(BF)

    def z_landed(it, e, cond_y=None):
        for side in range(2):
            cond = z_has[side] if cond_y is None else z_has[side] & cond_y
            @pl.when(cond)
            def _():
                for c in range(2):
                    landed(wi.at[it, side, c, e], it, z_sid(side, c, e), z_dev[side][c])

    def halo(it, e):
        for c in range(2):
            owners = pair if c == 0 else other
            pk[owners[0]], pk[owners[1]] = by_side(wi[it, 0, c, e], wi[it, 1, c, e])
        base = pl.multiple_of(e * blk, blk)
        for x in range(planes):
            rim = jnp.where(group_h % own == x % own, pk[x // own], 0.0)
            fb[pl.ds(base + x * hw, hw), rows_z:] = rim.astype(BF)

    def rim_forward(it):
        for u, e, name in ((0, 0, "yd"), (1, nb + 1, "yu")):
            @pl.when(y_has[u])
            def _():
                for k in range(2):
                    landed(fg.at[it, e, mine(pair[k])], it, sid[name] + k, y_to[u])
                    core_send(it, e, k)

    def rim_gather(it, e):
        @pl.when(used(e))
        def _():
            gather(it, e)
            z_landed(it, e, used(e))
            halo(it, e)

    def forward(e):
        b = e - 1
        base = pl.multiple_of(b * blk, blk)
        g = jnp.dot(am[...], fb[pl.ds(base, 3 * blk), :], preferred_element_type=F32).astype(BF)
        z_block = lax.broadcasted_iota(jnp.int32, (1, rows_z), 1) // BZ
        y_block = b * hw // BY
        for vv in range(views):
            scale = jnp.zeros((1, rows_z), F32)
            valid = jnp.zeros((1, rows_z), jnp.int32)
            for c in range(rows_z // BZ):
                scale = jnp.where(z_block == c, scales[vv, y_block, c], scale)
                valid = jnp.where(z_block == c, flags[vv, y_block, c], valid)
            blurred = lax.dot_general(
                g[vv * blk : (vv + 1) * blk], mt[vv], (((1,), (1,)), ((), ())),
                preferred_element_type=F32,
            )
            data = vd[vv, :, pl.ds(pl.multiple_of(b * hw, hw), hw), :].astype(F32)
            ratio = jnp.where(
                valid == 1, data.reshape(blk, rows_z) * (scale * gains[vv][0]) / blurred, 1.0
            )
            spread = jnp.dot((ratio * gains[vv][1]).astype(BF), mt[vv], preferred_element_type=F32)
            spread = spread.astype(BF)
            gp[vv, pl.ds(base + 2 * blk, blk), :] = spread[:, :rows_z]
            gh[vv, pl.ds(base + 2 * blk, blk), :LANES] = spread[:, rows_z:]
            gh[vv, pl.ds(base + blk, blk), LANES:] = spread[:, rows_z:]

    def r1_copy(it, e, k):
        return rcopy(ob.at[it, e, mine(other[k])], r1.at[it, e, k], it, sid["r1"] + 2 * e + k, to_a)

    def back(it, e):
        rows = pl.ds(pl.multiple_of(e * blk, blk), 3 * blk)
        total = jnp.dot(bm[0], gp[0, rows, :], preferred_element_type=F32)
        for vv in range(1, views):
            total = total + jnp.dot(bm[vv], gp[vv, rows, :], preferred_element_type=F32)
        ob[it, e] = total.reshape(planes, hw, rows_z)
        for k in range(2):
            r1_copy(it, e, k).start()

    def z_rims(it):
        for e in range(0, ne, 2):
            rows = slice(e * blk, (e + 3) * blk)
            total = jnp.dot(bm[0], gh[0, rows, :], preferred_element_type=F32)
            for vv in range(1, views):
                total = total + jnp.dot(bm[vv], gh[vv, rows, :], preferred_element_type=F32)
            rims = total.reshape(planes, hw, 2 * LANES)
            for n in range(2):
                for o in range(planes // own):
                    packed = rims[own * o, :, n * LANES : (n + 1) * LANES]
                    for p in range(1, own):
                        rim = rims[own * o + p, :, n * LANES : (n + 1) * LANES]
                        packed = jnp.where(group_h % own == p, rim, packed)
                    zp[it, o, e + n] = packed
        for k in range(2):
            rcopy(zp.at[it, other[k]], r1z.at[it, k], it, sid["r1z"] + k, to_a).start()

    zb_kinds = (
        (slice(1, nb + 1), None, slice(1, nb + 1)),
        (slice(0, 1), 0, slice(nb + 1, nb + 2)),
        (slice(nb + 1, nb + 2), 1, slice(0, 1)),
    )

    def each_zb(fn, landing=False):
        for d in range(2):
            for n, (src, u, dst) in enumerate(zb_kinds):
                u = 1 - u if landing and u is not None else u
                cond = z_has[d] if u is None else z_has[d] & y_has[u]
                dev = z_dev[d][0] if u is None else dict(z_dev[d][0], gy=y_co[u])
                @pl.when(cond)
                def _():
                    fn(d, n, src, dst, dev)

    def z_rims_send(it):
        for k in range(2):
            landed(r1z.at[it, k], it, sid["r1z"] + k, to_a)
        for e in range(ne):
            zo[it, 0, e], zo[it, 1, e] = by_side(
                zp[it, v, e] + r1z[it, 0, e], zp[it, vb, e] + r1z[it, 1, e]
            )
        each_zb(lambda d, n, src, dst, dev: rcopy(
            zo.at[it, d, src], zi.at[it, 1 - d, dst], it, sid["zb"] + 3 * (1 - d) + n, dev
        ).start())

    def z_rims_take(it, order, raw):
        each_zb(lambda d, n, src, dst, dev: landed(
            zi.at[it, d, dst], it, sid["zb"] + 3 * d + n, dev), True)
        for e in range(1, nb + 1):
            lf, rt = (zi[it, 0, e], zi[it, 1, e])
            if e == 1:
                lf, rt = (lf + zi[it, 0, 0], rt + zi[it, 1, 0])
            if e == nb:
                lf, rt = (lf + zi[it, 0, nb + 1], rt + zi[it, 1, nb + 1])
            zt[it, 0, e], zt[it, 1, e] = by_side(lf, rt)
        last = it + 1 == ITERS
        for n in range(raw):
            zx[it, 0, n] = zt[it, 1, order[n]]
            zx[it, 1, n] = zt[it, 0, order[n]]
        for k in range(1 if last else 2):
            rcopy(zx.at[it, k, :raw], zr.at[it, k, :raw], it, sid["zx"] + k, to_b).start()

    def side_parts(tile, p):
        first = roll_lanes(tile, -hw * p)
        final = roll_lanes(tile, LANES - hw - half - hw * p)
        return jnp.where(lane_h < hw, first, 0.0), jnp.where(lane_h >= LANES - hw, final, 0.0)

    def rim_finish(it, e):
        for k in range(2):
            r1_copy(it, e, k).wait_recv()
            tt[it, e, k] = ob[it, e, mine(pair[k])] + r1[it, e, k]
            for u, e_from in ((0, 0), (1, nb + 1)):
                @pl.when(y_has[u] & (e == e_from))
                def _():
                    rcopy(
                        tt.at[it, e_from, k], yi.at[it, 1 - u, k], it,
                        sid["yb"] + 2 * (1 - u) + k, y_to[u],
                    ).start()

    def finish(it, e, edge, with_rims):
        last = it + 1 == ITERS
        for k in (1, 0):
            r1_copy(it, e, k).wait_recv()
            tt[it, e, k] = ob[it, e, mine(pair[k])] + r1[it, e, k]
            if edge:
                for u, e_to in ((0, 1), (1, nb)):
                    @pl.when(y_has[u] & (e == e_to))
                    def _():
                        landed(yi.at[it, u, k], it, sid["yb"] + 2 * u + k, y_to[u])
                        tt[it, e, k] = tt[it, e, k] + yi[it, u, k]
            if with_rims:
                for p in range(own):
                    first, final = side_parts(zt[it, k, e], p)
                    tt[it, e, k, p, :, :LANES] += first
                    tt[it, e, k, p, :, rows_z - LANES :] += final
            if k == 1 or not last:
                rcopy(tt.at[it, e, k], r2.at[it, e, 1 - k], it, sid["r2"] + 2 * e + 1 - k, to_b).start()

    def corrected(it, e, k, n, raw):
        landed(r2.at[it, e, k], it, sid["r2"] + 2 * e + k, to_b)
        tile = zt[it, k, e] + zr[it, k, n] if n < raw else None
        for p in range(own):
            total = tt[it, e, k, p] + r2[it, e, k, p]
            if tile is not None:
                first, final = side_parts(tile, p)
                total = jnp.concatenate([
                    total[:, :LANES] + first, total[:, LANES : rows_z - LANES],
                    total[:, rows_z - LANES :] + final,
                ], axis=1) if rows_z > 2 * LANES else jnp.concatenate(
                    [total[:, :LANES] + first, total[:, LANES:] + final], axis=1)
            yield p, fg[it, e, own * pair[k] + p] * total / view_total

    def m(e):
        return flipped(e)

    load_order = [m(e) for e in range(nb, 0, -1)]
    x_send(load_order[0])
    core_send(0, load_order[0], 0)
    y_send(0, m(nb), (0,))
    y_send(0, m(1), (0,))
    for e in range(1, nb + 1):
        edges(0, e, 0)
    rcopy(et.at[0, 0, main], et.at[0, 1, main], 0, sid["x"], to_b).start()
    for e in load_order[1:]:
        x_send(e)
        core_send(0, e, 0)

    with scope("build"):
        for c in small:
            c.wait()
        build_taps(taps, profile, supports, views)
        for vv in range(views):
            build_depth(mt, vv, taps[0, 3 * vv + 2 : 3 * vv + 3, :], rows_z, hw)
            build_plane_row(
                am, vv * blk, taps[0, 3 * vv : 3 * vv + 1, :],
                taps[0, 3 * vv + 1 : 3 * vv + 2, :], planes, hw,
            )
        for e in (0, nb + 1):
            fb[e * blk : (e + 1) * blk, :] = jnp.zeros((blk, rows_z + LANES), BF)
    gains = []

    def build_backward():
        for vv in range(views):
            build_plane_row(
                bm.at[vv], 0, taps[1, 3 * vv : 3 * vv + 1, :],
                taps[1, 3 * vv + 1 : 3 * vv + 2, :], planes, hw,
            )
            for e in (0, 1, nb + 2, nb + 3):
                gp[vv, e * blk : (e + 1) * blk, :] = jnp.zeros((blk, rows_z), BF)
                gh[vv, e * blk : (e + 1) * blk, :LANES] = jnp.zeros((blk, LANES), BF)
            for e in (-1, 0, nb + 1, nb + 2, nb + 3):
                if e >= 0:
                    gh[vv, e * blk : (e + 1) * blk, LANES:] = jnp.zeros((blk, LANES), BF)
        for vv in range(views):
            mid = planes // 2 * hw
            along_z = mt[vv, rows_z // 2 : rows_z // 2 + 1, :rows_z].astype(F32)
            along_z = jnp.sum(along_z, axis=1, keepdims=True)
            fwd = am[vv * blk + mid : vv * blk + mid + 1, :].astype(F32)
            bwd = bm[vv, mid : mid + 1, :].astype(F32)
            gains.append((
                jnp.sum(fwd, axis=1, keepdims=True) * along_z,
                1.0 / (jnp.sum(bwd, axis=1, keepdims=True) * along_z),
            ))

    def raw_of(it):
        return nb if it + 1 == ITERS else 2

    def load_first(e):
        landed(fg.at[0, e, mine(vb)], 0, sid["x"] + e, to_b)
        core_send(0, e, 1)

    def step_order(it):
        mid_order = [m(nb - 1), m(nb)] + [m(e) for e in range(nb - 2, 0, -1)]
        last_order = [m(e) for e in range(nb - 1, 0, -1)] + [m(nb)]
        return last_order if it + 1 == ITERS else mid_order

    def prepare_first(i):
        if i == 0:
            load_first(load_order[0])
            y_send(0, load_order[0], (1,))
            landed(et.at[0, 1, main], 0, sid["x"], to_b)
            for e in range(1, nb + 1):
                z_split(0, e)
            for d in range(2):
                for c in range(2):
                    @pl.when(z_has[d])
                    def _():
                        rcopy(
                            wk.at[0, d, main], wi.at[0, 1 - d, c, main], 0, z_sid(1 - d, c, 1), z_dev[d][c]
                        ).start()
            diag_send(0, 1)
            diag_send(0, nb)
            build_backward()
            for e in load_order[1:-1]:
                load_first(e)
            rim_forward(0)
            for side in range(2):
                @pl.when(z_has[side])
                def _():
                    for c in range(2):
                        landed(wi.at[0, side, c, main], 0, z_sid(side, c, 1), z_dev[side][c])
            for e in load_order[:-1]:
                gather(0, e)
                halo(0, e)
            load_first(load_order[-1])
            y_send(0, load_order[-1], (1,))
            halo(0, load_order[-1])
            rim_gather(0, m(nb + 1))
            load.wait()
        elif i == 2:
            gather(0, load_order[-1])
        elif i == 3:
            rim_gather(0, m(0))

    def update(it, n):
        order = step_order(it - 1)
        e = order[n]
        raw = raw_of(it - 1)
        if n == 0:
            for k in range(2):
                landed(zr.at[it - 1, k, :raw], it - 1, sid["zx"] + k, to_b)
        for k in range(2):
            for p, fresh in corrected(it - 1, e, k, n, raw):
                fg[it, e, own * pair[k] + p] = fresh
            core_send(it, e, k)
            edges(it, e, k)
        y_send(it, e, (0, 1))
        z_split(it, e)
        z_send(it, e)
        diag_send(it, e)

    def prepare_next(it, i):
        order = step_order(it - 1)
        if i == 0:
            for n in range(nb):
                with scope("update"):
                    update(it, n)
                if n:
                    gather(it, order[n - 1])
                    z_landed(it, order[n - 1])
                    halo(it, order[n - 1])
        elif i == 1:
            rim_forward(it)
            rim_gather(it, m(nb + 1))
        elif i == 2:
            gather(it, order[nb - 1])
            z_landed(it, order[nb - 1])
            halo(it, order[nb - 1])
        elif i == 3:
            rim_gather(it, m(0))

    for it in range(ITERS):
        last = it + 1 == ITERS
        order = step_order(it)
        raw = raw_of(it)
        top = (nb, nb - 1) if it == 0 else (nb - 1, nb)
        rim = m(nb + 1)
        far = m(0)
        with scope(f"prep{it}0"):
            prepare_first(0) if it == 0 else prepare_next(it, 0)

        @pl.loop(0, nb)
        def _(i):
            for n in range(1, 4):
                @pl.when(i == n)
                def _():
                    with scope(f"prep{it}{n}"):
                        prepare_first(n) if it == 0 else prepare_next(it, n)
            e = jnp.where(i == 0, top[0], jnp.where(i == 1, top[1], nb - i))
            with scope(f"fwd{it}"):
                forward(m(e))

            @pl.when((e == nb) & used(rim))
            def _():
                with scope(f"rimb{it}"):
                    back(it, rim)

            @pl.when((i == (1 if it == 0 else 2)) & used(rim))
            def _():
                with scope(f"rimfin{it}"):
                    rim_finish(it, rim)

            @pl.when(i == 2)
            def _():
                with scope(f"back{it}"):
                    back(it, order[0])

        with scope(f"tail{it}"):
            @pl.when(used(far))
            def _():
                back(it, far)
            back(it, order[1])
            with scope(f"fin{it}"):
                finish(it, order[0], False, False)
            with scope(f"zrim{it}"):
                z_rims(it)

            @pl.when(used(far))
            def _():
                rim_finish(it, far)
            back(it, order[2])
            if last:
                with scope(f"fin{it}"):
                    finish(it, order[1], False, False)
            with scope(f"zrs{it}"):
                z_rims_send(it)
            if not last:
                with scope(f"fin{it}"):
                    finish(it, order[1], True, False)
            for n in range(3, nb):
                back(it, order[n])
            if last:
                for n in range(2, nb):
                    with scope(f"fin{it}"):
                        finish(it, order[n], n >= nb - 2, False)
                with scope(f"zrt{it}"):
                    z_rims_take(it, order, raw)
            else:
                with scope(f"zrt{it}"):
                    z_rims_take(it, order, raw)
                for n in range(2, nb):
                    with scope(f"fin{it}"):
                        finish(it, order[n], n == nb - 1, True)

        if last:
            for n in range(nb):
                with scope("final"):
                    e = order[n]
                    if n == 0:
                        landed(zr.at[it, 0, :raw], it, sid["zx"], to_b)
                    for p, fresh in corrected(it, e, 0, n, raw):
                        out[p, pl.ds(pl.multiple_of((e - 1) * hw, hw), hw), :] = fresh

    for it in range(ITERS):
        last = it + 1 == ITERS
        raw = raw_of(it)
        if it == 0:
            sent(et.at[0, 0, main], 0, sid["x"], to_b)
            for e in range(1, nb + 1):
                sent(fg.at[0, e, mine(v)], 0, sid["x"] + e, to_b)
        for d in range(2):
            @pl.when(z_has[d])
            def _():
                for c in range(2):
                    if it == 0:
                        sent(wk.at[it, d, main], it, z_sid(1 - d, c, 1), z_dev[d][c])
                    else:
                        for e in range(1, nb + 1):
                            sent(wk.at[it, d, e], it, z_sid(1 - d, c, e), z_dev[d][c])
            for u, e_from, e_to in ((0, 1, nb + 1), (1, nb, 0)):
                @pl.when(z_has[d] & y_has[u])
                def _():
                    for c in range(2):
                        sent(
                            wk.at[it, d, e_from], it, z_sid(1 - d, c, e_to),
                            dict(z_dev[d][c], gy=y_co[u]),
                        )
        each_zb(lambda d, n, src, dst, dev: sent(
            zo.at[it, d, src], it, sid["zb"] + 3 * (1 - d) + n, dev))
        for u, e, name in ((0, 1, "yu"), (1, nb, "yd")):
            @pl.when(y_has[u])
            def _():
                for k in range(2):
                    sent(fg.at[it, e, mine(pair[k])], it, sid[name] + k, y_to[u])
                    rim = 0 if u == 0 else nb + 1
                    sent(tt.at[it, rim, k], it, sid["yb"] + 2 * (1 - u) + k, y_to[u])
        for k in range(2):
            sent(zp.at[it, other[k]], it, sid["r1z"] + k, to_a)
        for k in range(1 if last else 2):
            sent(zx.at[it, k, :raw], it, sid["zx"] + k, to_b)

        @pl.loop(0, ne)
        def _(e):
            @pl.when(used(e))
            def _():
                for k in range(2):
                    sent(fg.at[it, e, mine(pair[k])], it, sid["core"] + 2 * e + k, to_a)
                    r1_copy(it, e, k).wait_send()

            @pl.when((e > 0) & (e < nb + 1))
            def _():
                for k in range(2):
                    if k == 1 or not last:
                        sent(tt.at[it, e, k], it, sid["r2"] + 2 * e + 1 - k, to_b)


def per_device(ny, nz, estimate, view_data, block_scales, block_flags, profile, supports):
    views, planes, rows_y, rows_z = view_data.shape
    own = estimate.shape[0]
    hw = (profile.shape[2] - 1) // 2
    nb = rows_y // hw
    ne = nb + 2
    blk = planes * hw
    wide = rows_z + LANES
    tap_rows = -(-3 * views // 8) * 8
    owners = planes // own
    _, n_sem = sem_bases(ne)
    n = ITERS
    vm = pltpu.VMEM
    table = jnp.transpose(profile, (1, 0, 2))
    scratch = [
        pltpu.SMEM(block_scales.shape, F32),
        pltpu.SMEM(block_flags.shape, jnp.int32),
        vm(table.shape, F32),
        pltpu.SMEM(supports.shape, jnp.int32),
        vm((2, tap_rows, LANES), F32),
        vm((n, ne, planes, hw, rows_z), F32),
        vm((ne * blk, wide), BF),
        vm((views * blk, 3 * blk), BF),
        vm((views, blk, 3 * blk), BF),
        vm((views, rows_z, wide), BF),
        vm((views, (nb + 4) * blk, rows_z), BF),
        vm((views, (nb + 4) * blk, 2 * LANES), BF),
        vm((n, ne, planes, hw, rows_z), F32),
        vm((n, ne, 2, own, hw, rows_z), F32),
        vm((n, ne, 2, own, hw, rows_z), F32),
        vm((n, ne, 2, own, hw, rows_z), F32),
        vm((n, 2, 2, own, hw, rows_z), F32),
        vm((n, 2, ne, hw, LANES), F32),
        vm((n, 2, ne, hw, LANES), F32),
        vm((n, 2, 2, ne, hw, LANES), F32),
        vm((owners, hw, LANES), F32),
        vm((n, owners, ne, hw, LANES), F32),
        vm((n, 2, ne, hw, LANES), F32),
        vm((n, 2, ne, hw, LANES), F32),
        vm((n, 2, ne, hw, LANES), F32),
        vm((n, 2, ne, hw, LANES), F32),
        vm((n, 2, nb, hw, LANES), F32),
        vm((n, 2, nb, hw, LANES), F32),
        vm(view_data.shape, view_data.dtype),
        pltpu.SemaphoreType.DMA((5 + nb,)),
        pltpu.SemaphoreType.DMA((n, n_sem)),
        pltpu.SemaphoreType.DMA((n, n_sem)),
    ]
    in_hbm = pl.BlockSpec(memory_space=pltpu.HBM)
    return pl.pallas_call(
        functools.partial(kernel, (ny, nz, views, planes, rows_y, rows_z, own, hw)),
        out_shape=jax.ShapeDtypeStruct(estimate.shape, F32),
        in_specs=[in_hbm] * 6,
        out_specs=pl.BlockSpec(memory_space=pltpu.VMEM),
        scratch_shapes=scratch,
        compiler_params=pltpu.CompilerParams(
            collective_id=0, has_side_effects=True, vmem_limit_bytes=62 * 1024 * 1024
        ),
    )(estimate, view_data, block_scales, block_flags, table, supports)


def solution(mesh):
    placed = (
        P("view", "gy", "gz"),
        P("view", None, "gy", "gz"),
        P("view", "gy", "gz"),
        P("view", "gy", "gz"),
        P("view", None, None),
        P("view", None),
    )
    body = functools.partial(per_device, mesh.shape["gy"], mesh.shape["gz"])
    return jax.shard_map(
        body, mesh=mesh, in_specs=placed, out_specs=P("view", "gy", "gz"), check_vma=False
    )
```

```python
import contextlib
import functools

import jax
import jax.numpy as jnp
from jax import lax
from jax.experimental import pallas as pl
from jax.experimental.pallas import tpu as pltpu
from jax.sharding import PartitionSpec as P

BY = 32
BZ = 64
ITERS = 2
LANES = 128
MESH = pl.DeviceIdType.MESH
BF = jnp.bfloat16
F32 = jnp.float32


def scope(name):
    return contextlib.nullcontext()


def lane_iota(rows):
    return lax.broadcasted_iota(jnp.int32, (rows, LANES), 1)


def toeplitz(row, rows, shift):
    wide = jnp.broadcast_to(row, (rows, LANES))
    return pltpu.roll(wide, shift % LANES, 1, stride=1, stride_axis=0)


def roll_lanes(x, shift):
    shift = shift % LANES
    return pltpu.roll(x, shift, x.ndim - 1) if shift else x


def build_taps(dst, profile, supports, views):
    taps = profile.shape[2]
    dst[...] = jnp.zeros_like(dst)
    for vv in range(views):
        for a in range(3):
            r = 3 * vv + a
            dst[0, r : r + 1, :taps] = profile[a, vv : vv + 1, :]
    rows = dst.shape[1]
    row = lax.broadcasted_iota(jnp.int32, (rows, LANES), 0)
    lane = lane_iota(rows)
    reach = jnp.zeros((rows, LANES), jnp.int32)
    for vv in range(views):
        for a in range(3):
            reach = jnp.where(row == 3 * vv + a, supports[vv, a], reach)
    inside = (jnp.abs(lane - (taps - 1) // 2) <= reach) & (row < 3 * views)
    masked = jnp.where(inside, dst[0], 0.0)
    total = jnp.sum(masked, axis=1, keepdims=True)
    table = masked / jnp.where(total > 0.0, total, 1.0)
    turn = lax.broadcasted_iota(jnp.int32, (LANES, LANES), 0) + lax.broadcasted_iota(
        jnp.int32, (LANES, LANES), 1
    )
    flip = (turn == taps - 1).astype(F32)
    dst[0] = table
    dst[1] = jnp.dot(table, flip, precision=lax.Precision.HIGHEST, preferred_element_type=F32)


def build_plane_row(dst, row_base, kx, ky, planes, hw):
    lane = lane_iota(hw)
    per_tile = LANES // hw
    halves = planes // per_tile
    tall = toeplitz(ky, hw, 0)
    bands = []
    for d in range(3):
        q = jnp.where(lane < hw, roll_lanes(tall, -hw * d), 0.0)
        width = hw
        while width < LANES:
            q = q + roll_lanes(q, width)
            width *= 2
        bands.append(q)
    tx = toeplitz(kx, planes, -hw)
    row_id = lax.broadcasted_iota(jnp.int32, (LANES, LANES), 0)
    group = lax.broadcasted_iota(jnp.int32, (LANES, LANES), 1) // hw
    for half in range(halves):
        pick = (row_id == group + half * per_tile).astype(F32)
        spread = jnp.dot(tx, pick, precision=lax.Precision.HIGHEST, preferred_element_type=F32)
        for d in range(3):
            for x in range(planes):
                tile = spread[x : x + 1, :] * bands[d]
                c0 = (halves * d + half) * LANES
                dst[row_base + x * hw : row_base + (x + 1) * hw, c0 : c0 + LANES] = tile.astype(BF)


def build_depth(dst, v, kz, rows_z, hw):
    row_j = lax.broadcasted_iota(jnp.int32, (rows_z, LANES), 0)
    lane = lane_iota(rows_z)
    reps = rows_z // LANES
    t = jnp.concatenate([toeplitz(kz, LANES, -hw)] * reps, axis=0)
    for ct in range(reps):
        c = lane + ct * LANES
        keep = jnp.abs(c - row_j) <= hw
        dst[v, :, ct * LANES : (ct + 1) * LANES] = jnp.where(keep, t, 0.0).astype(BF)
    h = jnp.concatenate([toeplitz(kz, LANES, 0)] * reps, axis=0)
    low = (row_j < hw) & (lane < hw)
    high = (row_j >= rows_z - hw) & (lane >= hw) & (lane < 2 * hw)
    h = jnp.where(low, h, 0.0) + roll_lanes(jnp.where(high, h, 0.0), LANES // 2 - hw)
    width = hw
    while width < LANES // 2:
        h = h + roll_lanes(h, width)
        width *= 2
    dst[v, :, rows_z : rows_z + LANES] = h.astype(BF)


def sem_bases(ne):
    names = [
        ("x", ne), ("core", ne), ("y", 2), ("z", 2 * ne), ("r1", ne), ("r1z", 1), ("zb", 6),
        ("yb", 2), ("r2", ITERS * ne), ("zx", ITERS),
    ]
    bases, count = {}, 0
    for name, size in names:
        bases[name] = count
        count += size
    return bases, count


def kernel(
    sizes, est, vd_any, scales_any, flags_any, profile_any, supports_any, out,
    scales, flags, profile, supports, taps,
    fg, fb, am, bm, mt, gp, gh, ob, r1, tt, r2, yi, et, wk, wi, pk, zp, r1z, zo, zi, zt, zx, zr, vd, count,
    lsem, ssem, rsem,
):
    ny, nz, views, planes, rows_y, rows_z, own, hw = sizes
    nb = rows_y // hw
    ne = nb + 2
    blk = planes * hw
    half = LANES // 2
    v = lax.axis_index("view")
    gy = lax.axis_index("gy")
    gz = lax.axis_index("gz")
    va, vb, vc = (lax.bitwise_xor(v, 1), lax.bitwise_xor(v, 2), lax.bitwise_xor(v, 3))
    has_up, has_dn = (gy > 0, gy < ny - 1)
    has_lf, has_rt = (gz > 0, gz < nz - 1)
    yup, ydn = (jnp.maximum(gy - 1, 0), jnp.minimum(gy + 1, ny - 1))
    zlf, zrt = (jnp.maximum(gz - 1, 0), jnp.minimum(gz + 1, nz - 1))
    to_a, to_b = ({"view": va}, {"view": vb})
    to_up, to_dn = ({"gy": yup}, {"gy": ydn})
    to_lf, to_rt = ({"gz": zlf}, {"gz": zrt})
    z_dev = [[to_lf, {"gz": zlf, "view": va}], [to_rt, {"gz": zrt, "view": va}]]
    z_has = [has_lf, has_rt]
    y_has = [has_up, has_dn]
    y_to = [to_up, to_dn]
    y_co = [yup, ydn]
    z_co = [zlf, zrt]
    view_total = views * 4
    pair = (v, vb)
    other = (va, vc)
    sid, _ = sem_bases(ne)

    def mine(o):
        return pl.ds(o * own, own)

    def rcopy(src, dst, s, group, dev):
        return pltpu.make_async_remote_copy(
            src_ref=src, dst_ref=dst, send_sem=ssem.at[group], recv_sem=rsem.at[s],
            device_id=dev, device_id_type=MESH,
        )

    def landed(dst, s, dev):
        rcopy(dst, dst, s, 0, dev).wait_recv()

    def y_group(u):
        return 1 + u

    def z_group(d):
        return 3 + d

    def diag_group(d, u):
        return 5 + 2 * d + u

    def flipped(e):
        return jnp.where(has_dn, e, nb + 1 - e)

    def used(e):
        return ((e > 0) | has_up) & ((e < nb + 1) | has_dn)

    est_load = [
        pltpu.make_async_copy(
            est.at[:, b * hw : (b + 1) * hw, :], fg.at[0, b + 1, mine(v)], lsem.at[5 + b]
        )
        for b in range(nb)
    ]
    small = [
        pltpu.make_async_copy(s, d, lsem.at[i])
        for i, (s, d) in enumerate((
            (profile_any, profile), (supports_any, supports), (scales_any, scales), (flags_any, flags),
        ))
    ]
    load = pltpu.make_async_copy(vd_any, vd, lsem.at[4])
    for c in est_load:
        c.start()
    for c in small:
        c.start()
    load.start()

    barrier = pltpu.get_barrier_semaphore()
    meets = [(None, to_a), (None, to_b), (has_up, to_up), (has_dn, to_dn)]
    for d in range(2):
        for c in range(2):
            meets.append((z_has[d], z_dev[d][c]))
            for u in range(2):
                dev = dict(z_dev[d][c], gy=y_co[u])
                meets.append((z_has[d] & y_has[u], dev))
    expected = jnp.int32(0)
    for cond, dev in meets:
        if cond is None:
            pl.semaphore_signal(barrier, inc=1, device_id=dev, device_id_type=MESH)
            expected = expected + 1
        else:
            @pl.when(cond)
            def _():
                pl.semaphore_signal(barrier, inc=1, device_id=dev, device_id_type=MESH)
            expected = expected + cond.astype(jnp.int32)

    for d in range(2):
        @pl.when(jnp.logical_not(z_has[d]))
        def _():
            for it in range(ITERS):
                for c in range(2):
                    wi[it, d, c] = jnp.zeros((ne, hw, LANES), F32)
                zi[it, d] = jnp.zeros((ne, hw, LANES), F32)

        for u, e in ((0, 0), (1, nb + 1)):
            @pl.when(z_has[d] & jnp.logical_not(y_has[u]))
            def _():
                for it in range(ITERS):
                    zi[it, d, e] = jnp.zeros((hw, LANES), F32)

    for c in est_load:
        c.wait()

    def core_send(it, e, k, group=0):
        ref = fg.at[it, e, mine(pair[k])]
        rcopy(ref, ref, sid["core"] + e, group, to_a).start()

    def y_send(it, e, ks):
        for u, e_from, e_to in ((0, 1, nb + 1), (1, nb, 0)):
            @pl.when(y_has[u] & (e == e_from))
            def _():
                for k in ks:
                    rcopy(
                        fg.at[it, e_from, mine(pair[k])], fg.at[it, e_to, mine(pair[k])],
                        sid["y"] + 1 - u, y_group(u), y_to[u],
                    ).start()

    def x_send(e):
        ref = fg.at[0, e, mine(v)]
        rcopy(ref, ref, sid["x"] + e, 0, to_b).start()

    lane_h = lane_iota(hw)
    group_h = lane_h // hw
    main = slice(1, nb + 1)

    def edges(it, e, k):
        tile = jnp.zeros((hw, LANES), F32)
        for p in range(own):
            body = fg[it, e, own * pair[k] + p]
            tile = jnp.where(group_h == p, roll_lanes(body[:, :LANES], hw * p), tile)
            tile = jnp.where(
                group_h == own + p, roll_lanes(body[:, rows_z - LANES :], hw * (own + p + 1)), tile
            )
        et[it, k, e] = tile

    def by_side(near, far):
        return (
            jnp.where(lane_h < half, near, roll_lanes(far, half)),
            jnp.where(lane_h < half, roll_lanes(near, half), far),
        )

    def z_sid(side, e):
        return sid["z"] + side * ne + e

    def z_send(it, e):
        for d in range(2):
            for c in range(2):
                @pl.when(z_has[d])
                def _():
                    rcopy(wk.at[it, d, e], wi.at[it, 1 - d, c, e], z_sid(1 - d, e), z_group(d), z_dev[d][c]).start()

    def diag_send(it, e):
        for u, e_from, e_to in ((0, 1, nb + 1), (1, nb, 0)):
            for d in range(2):
                @pl.when(z_has[d] & y_has[u] & (e == e_from))
                def _():
                    for c in range(2):
                        rcopy(
                            wk.at[it, d, e_from], wi.at[it, 1 - d, c, e_to], z_sid(1 - d, e_to),
                            diag_group(d, u), dict(z_dev[d][c], gy=y_co[u]),
                        ).start()

    def z_split(it, e):
        wk[it, 0, e], wk[it, 1, e] = by_side(et[it, 0, e], et[it, 1, e])

    def gather(it, e):
        landed(fg.at[it, e, pl.ds(0, 2 * own)], sid["core"] + e, to_a)
        fb[pl.ds(pl.multiple_of(e * blk, blk), blk), :rows_z] = fg[it, e].reshape(blk, rows_z).astype(BF)

    def z_landed(it, e, cond_y=None):
        for side in range(2):
            cond = z_has[side] if cond_y is None else z_has[side] & cond_y
            @pl.when(cond)
            def _():
                landed(wi.at[it, side, :, e], z_sid(side, e), z_dev[side][0])

    def halo(it, e):
        for c in range(2):
            owners = pair if c == 0 else other
            pk[owners[0]], pk[owners[1]] = by_side(wi[it, 0, c, e], wi[it, 1, c, e])
        base = pl.multiple_of(e * blk, blk)
        for x in range(planes):
            rim = jnp.where(group_h % own == x % own, pk[x // own], 0.0)
            fb[pl.ds(base + x * hw, hw), rows_z:] = rim.astype(BF)

    def rim_forward(it):
        for u, e in ((0, 0), (1, nb + 1)):
            @pl.when(y_has[u])
            def _():
                landed(fg.at[it, e, pl.ds(0, 2 * own)], sid["y"] + u, y_to[u])
                for k in range(2):
                    core_send(it, e, k, y_group(u))

    def rim_gather(it, e):
        @pl.when(used(e))
        def _():
            gather(it, e)
            z_landed(it, e, used(e))
            halo(it, e)

    def forward(e):
        b = e - 1
        base = pl.multiple_of(b * blk, blk)
        g = jnp.dot(am[...], fb[pl.ds(base, 3 * blk), :], preferred_element_type=F32).astype(BF)
        z_block = lax.broadcasted_iota(jnp.int32, (1, rows_z), 1) // BZ
        y_block = b * hw // BY
        for vv in range(views):
            scale = jnp.zeros((1, rows_z), F32)
            valid = jnp.zeros((1, rows_z), jnp.int32)
            for c in range(rows_z // BZ):
                scale = jnp.where(z_block == c, scales[vv, y_block, c], scale)
                valid = jnp.where(z_block == c, flags[vv, y_block, c], valid)
            blurred = lax.dot_general(
                g[vv * blk : (vv + 1) * blk], mt[vv], (((1,), (1,)), ((), ())),
                preferred_element_type=F32,
            )
            data = vd[vv, :, pl.ds(pl.multiple_of(b * hw, hw), hw), :].astype(F32)
            ratio = jnp.where(
                valid == 1, data.reshape(blk, rows_z) * (scale * gains[vv][0]) / blurred, 1.0
            )
            spread = jnp.dot((ratio * gains[vv][1]).astype(BF), mt[vv], preferred_element_type=F32)
            spread = spread.astype(BF)
            gp[vv, pl.ds(base + 2 * blk, blk), :] = spread[:, :rows_z]
            gh[vv, pl.ds(base + 2 * blk, blk), :LANES] = spread[:, rows_z:]
            gh[vv, pl.ds(base + blk, blk), LANES:] = spread[:, rows_z:]

    def r1_send(it, e, group=0):
        for k in range(2):
            rcopy(ob.at[it, e, mine(other[k])], r1.at[it, e, k], sid["r1"] + e, group, to_a).start()

    def back(it, e, rim=False):
        rows = pl.ds(pl.multiple_of(e * blk, blk), 3 * blk)
        total = jnp.dot(bm[0], gp[0, rows, :], preferred_element_type=F32)
        for vv in range(1, views):
            total = total + jnp.dot(bm[vv], gp[vv, rows, :], preferred_element_type=F32)
        ob[it, e] = total.reshape(planes, hw, rows_z)
        if not rim:
            r1_send(it, e)
        else:
            for u, e_rim in ((0, 0), (1, nb + 1)):
                @pl.when(e == e_rim)
                def _():
                    r1_send(it, e_rim, y_group(u))

    def z_rims(it):
        for e in range(0, ne, 2):
            rows = slice(e * blk, (e + 3) * blk)
            total = jnp.dot(bm[0], gh[0, rows, :], preferred_element_type=F32)
            for vv in range(1, views):
                total = total + jnp.dot(bm[vv], gh[vv, rows, :], preferred_element_type=F32)
            rims = total.reshape(planes, hw, 2 * LANES)
            for n in range(2):
                for o in range(planes // own):
                    packed = rims[own * o, :, n * LANES : (n + 1) * LANES]
                    for p in range(1, own):
                        rim = rims[own * o + p, :, n * LANES : (n + 1) * LANES]
                        packed = jnp.where(group_h % own == p, rim, packed)
                    zp[it, o, e + n] = packed
        for k in range(2):
            rcopy(zp.at[it, other[k]], r1z.at[it, k], sid["r1z"], 0, to_a).start()

    zb_kinds = (
        (slice(1, nb + 1), None, slice(1, nb + 1)),
        (slice(0, 1), 0, slice(nb + 1, nb + 2)),
        (slice(nb + 1, nb + 2), 1, slice(0, 1)),
    )

    def each_zb(fn, landing=False):
        for d in range(2):
            for n, (src, u, dst) in enumerate(zb_kinds):
                u = 1 - u if landing and u is not None else u
                cond = z_has[d] if u is None else z_has[d] & y_has[u]
                dev = z_dev[d][0] if u is None else dict(z_dev[d][0], gy=y_co[u])
                @pl.when(cond)
                def _():
                    fn(d, n, src, dst, z_group(d) if u is None else diag_group(d, u), dev)

    def z_rims_send(it):
        landed(r1z.at[it], sid["r1z"], to_a)
        for e in range(ne):
            zo[it, 0, e], zo[it, 1, e] = by_side(
                zp[it, v, e] + r1z[it, 0, e], zp[it, vb, e] + r1z[it, 1, e]
            )
        each_zb(lambda d, n, src, dst, group, dev: rcopy(
            zo.at[it, d, src], zi.at[it, 1 - d, dst], sid["zb"] + 3 * (1 - d) + n, group, dev
        ).start())

    def z_rims_take(it, order, raw):
        each_zb(lambda d, n, src, dst, group, dev: landed(
            zi.at[it, d, dst], sid["zb"] + 3 * d + n, dev), True)
        for e in range(1, nb + 1):
            lf, rt = (zi[it, 0, e], zi[it, 1, e])
            if e == 1:
                lf, rt = (lf + zi[it, 0, 0], rt + zi[it, 1, 0])
            if e == nb:
                lf, rt = (lf + zi[it, 0, nb + 1], rt + zi[it, 1, nb + 1])
            zt[it, 0, e], zt[it, 1, e] = by_side(lf, rt)
        last = it + 1 == ITERS
        for n in range(raw):
            zx[it, 0, n] = zt[it, 1, order[n]]
            zx[it, 1, n] = zt[it, 0, order[n]]
        for k in range(1 if last else 2):
            rcopy(zx.at[it, k, :raw], zr.at[it, k, :raw], sid["zx"] + it, 0, to_b).start()

    def side_parts(tile, p):
        first = roll_lanes(tile, -hw * p)
        final = roll_lanes(tile, LANES - hw - half - hw * p)
        return jnp.where(lane_h < hw, first, 0.0), jnp.where(lane_h >= LANES - hw, final, 0.0)

    def rim_finish(it, e):
        landed(r1.at[it, e], sid["r1"] + e, to_a)
        for k in range(2):
            tt[it, e, k] = ob[it, e, mine(pair[k])] + r1[it, e, k]
        for u, e_from in ((0, 0), (1, nb + 1)):
            @pl.when(y_has[u] & (e == e_from))
            def _():
                rcopy(tt.at[it, e_from], yi.at[it, 1 - u], sid["yb"] + 1 - u, y_group(u), y_to[u]).start()

    def finish(it, e, edge, with_rims):
        last = it + 1 == ITERS
        landed(r1.at[it, e], sid["r1"] + e, to_a)
        if edge:
            for u, e_to in ((0, 1), (1, nb)):
                @pl.when(y_has[u] & (e == e_to))
                def _():
                    landed(yi.at[it, u], sid["yb"] + u, y_to[u])
        for k in (1, 0):
            tt[it, e, k] = ob[it, e, mine(pair[k])] + r1[it, e, k]
            if edge:
                for u, e_to in ((0, 1), (1, nb)):
                    @pl.when(y_has[u] & (e == e_to))
                    def _():
                        tt[it, e, k] = tt[it, e, k] + yi[it, u, k]
            if with_rims:
                for p in range(own):
                    first, final = side_parts(zt[it, k, e], p)
                    tt[it, e, k, p, :, :LANES] += first
                    tt[it, e, k, p, :, rows_z - LANES :] += final
            if k == 1 or not last:
                rcopy(tt.at[it, e, k], r2.at[it, e, 1 - k], sid["r2"] + it * ne + e, 0, to_b).start()

    def corrected(it, e, k, n, raw):
        tile = zt[it, k, e] + zr[it, k, n] if n < raw else None
        for p in range(own):
            total = tt[it, e, k, p] + r2[it, e, k, p]
            if tile is not None:
                first, final = side_parts(tile, p)
                total = jnp.concatenate([
                    total[:, :LANES] + first, total[:, LANES : rows_z - LANES],
                    total[:, rows_z - LANES :] + final,
                ], axis=1) if rows_z > 2 * LANES else jnp.concatenate(
                    [total[:, :LANES] + first, total[:, LANES:] + final], axis=1)
            yield p, fg[it, e, own * pair[k] + p] * total / view_total

    def m(e):
        return flipped(e)

    for e in range(1, nb + 1):
        edges(0, e, 0)
    with scope("barrier"):
        pl.semaphore_wait(barrier, expected)

    load_order = [m(e) for e in range(nb, 0, -1)]
    rcopy(et.at[0, 0, main], et.at[0, 1, main], sid["x"], 0, to_b).start()
    x_send(load_order[0])
    core_send(0, load_order[0], 0)
    y_send(0, m(nb), (0,))
    y_send(0, m(1), (0,))
    for e in load_order[1:]:
        x_send(e)
        core_send(0, e, 0)

    with scope("build"):
        for c in small:
            c.wait()
        build_taps(taps, profile, supports, views)
        for vv in range(views):
            build_depth(mt, vv, taps[0, 3 * vv + 2 : 3 * vv + 3, :], rows_z, hw)
            build_plane_row(
                am, vv * blk, taps[0, 3 * vv : 3 * vv + 1, :],
                taps[0, 3 * vv + 1 : 3 * vv + 2, :], planes, hw,
            )
        for e in (0, nb + 1):
            fb[e * blk : (e + 1) * blk, :] = jnp.zeros((blk, rows_z + LANES), BF)
    gains = []

    def build_backward():
        for vv in range(views):
            build_plane_row(
                bm.at[vv], 0, taps[1, 3 * vv : 3 * vv + 1, :],
                taps[1, 3 * vv + 1 : 3 * vv + 2, :], planes, hw,
            )
            for e in (0, 1, nb + 2, nb + 3):
                gp[vv, e * blk : (e + 1) * blk, :] = jnp.zeros((blk, rows_z), BF)
                gh[vv, e * blk : (e + 1) * blk, :LANES] = jnp.zeros((blk, LANES), BF)
            for e in (-1, 0, nb + 1, nb + 2, nb + 3):
                if e >= 0:
                    gh[vv, e * blk : (e + 1) * blk, LANES:] = jnp.zeros((blk, LANES), BF)
        for vv in range(views):
            mid = planes // 2 * hw
            along_z = mt[vv, rows_z // 2 : rows_z // 2 + 1, :rows_z].astype(F32)
            along_z = jnp.sum(along_z, axis=1, keepdims=True)
            fwd = am[vv * blk + mid : vv * blk + mid + 1, :].astype(F32)
            bwd = bm[vv, mid : mid + 1, :].astype(F32)
            gains.append((
                jnp.sum(fwd, axis=1, keepdims=True) * along_z,
                1.0 / (jnp.sum(bwd, axis=1, keepdims=True) * along_z),
            ))

    def raw_of(it):
        return nb if it + 1 == ITERS else 2

    def load_first(e):
        landed(fg.at[0, e, mine(vb)], sid["x"] + e, to_b)
        core_send(0, e, 1)

    def step_order(it):
        mid_order = [m(nb - 1), m(nb)] + [m(e) for e in range(nb - 2, 0, -1)]
        last_order = [m(e) for e in range(nb - 1, 0, -1)] + [m(nb)]
        return last_order if it + 1 == ITERS else mid_order

    def prepare_first(i):
        if i == 0:
            with scope('p_et'):
                landed(et.at[0, 1, main], sid["x"], to_b)
            for e in range(1, nb + 1):
                z_split(0, e)
            for d in range(2):
                for c in range(2):
                    @pl.when(z_has[d])
                    def _():
                        rcopy(
                            wk.at[0, d, main], wi.at[0, 1 - d, c, main], z_sid(1 - d, 1), z_group(d), z_dev[d][c]
                        ).start()
            diag_send(0, 1)
            diag_send(0, nb)
            with scope('p_first'):
                load_first(load_order[0])
            y_send(0, load_order[0], (1,))
            with scope("p_bb"):
                build_backward()
            for n, e in enumerate(load_order[1:-1]):
                with scope("p_x"):
                    load_first(e)
                gather(0, load_order[n])
                if n == 0:
                    for side in range(2):
                        @pl.when(z_has[side])
                        def _():
                            landed(wi.at[0, side, :, main], z_sid(side, 1), z_dev[side][0])
                    for q in load_order:
                        halo(0, q)
            with scope("p_rimf"):
                rim_forward(0)
            load.wait()
            with scope("p_gather"):
                gather(0, load_order[-2])
        elif i == 1:
            load_first(load_order[-1])
            y_send(0, load_order[-1], (1,))
            rim_gather(0, m(nb + 1))
        elif i == 2:
            gather(0, load_order[-1])
        elif i == 3:
            rim_gather(0, m(0))

    def update(it, n):
        order = step_order(it - 1)
        e = order[n]
        raw = raw_of(it - 1)
        if n == 0:
            landed(zr.at[it - 1, :, :raw], sid["zx"] + it - 1, to_b)
        landed(r2.at[it - 1, e], sid["r2"] + (it - 1) * ne + e, to_b)
        for k in range(2):
            for p, fresh in corrected(it - 1, e, k, n, raw):
                fg[it, e, own * pair[k] + p] = fresh
            core_send(it, e, k)
            edges(it, e, k)
        y_send(it, e, (0, 1))
        z_split(it, e)
        z_send(it, e)
        diag_send(it, e)

    def sends_done():
        plane, tile = rows_z // LANES, 1
        block = 2 * own * plane
        total = [0] * 9
        for it in range(ITERS):
            last = it + 1 == ITERS
            raw = raw_of(it)
            total[0] += nb * block * 2 + 2 * ne + nb * block // (2 if last else 1)
            total[0] += raw * (1 if last else 2)
            total[0] += nb * block // 2 + nb if it == 0 else 0
            for u in range(2):
                total[y_group(u)] += 4 * block
            for d in range(2):
                total[z_group(d)] += 2 * nb + nb
                for u in range(2):
                    total[diag_group(d, u)] += 3
        conds = [None, *y_has, *z_has, *(z_has[d] & y_has[u] for d in range(2) for u in range(2))]
        for group, (tiles, cond) in enumerate(zip(total, conds)):
            def done():
                ref = count.at[pl.ds(0, tiles)]
                rcopy(ref, ref, 0, group, to_a).wait_send()
            if cond is None:
                done()
            else:
                pl.when(cond)(done)

    def prepare_next(it, i):
        order = step_order(it - 1)
        if i == 0:
            for n in range(nb):
                with scope("update"):
                    update(it, n)
                if n == nb - 2:
                    for q in range(n):
                        gather(it, order[q])
                        z_landed(it, order[q])
                        halo(it, order[q])
                    gather(it, order[n])
                if n == nb - 1:
                    with scope("rimf"):
                        rim_forward(it)
                    with scope("halo"):
                        z_landed(it, order[n - 1])
                        halo(it, order[n - 1])
        elif i == 1:
            rim_gather(it, m(nb + 1))
        elif i == 2:
            gather(it, order[nb - 1])
            z_landed(it, order[nb - 1])
            halo(it, order[nb - 1])
        elif i == 3:
            rim_gather(it, m(0))

    for it in range(ITERS):
        last = it + 1 == ITERS
        order = step_order(it)
        raw = raw_of(it)
        top = (nb - 1, nb)
        rim = m(nb + 1)
        far = m(0)
        with scope(f"prep{it}0"):
            prepare_first(0) if it == 0 else prepare_next(it, 0)

        @pl.loop(0, nb)
        def _(i):
            for n in range(1, 4):
                @pl.when(i == n)
                def _():
                    with scope(f"prep{it}{n}"):
                        prepare_first(n) if it == 0 else prepare_next(it, n)
            e = jnp.where(i == 0, top[0], jnp.where(i == 1, top[1], nb - i))
            with scope(f"fwd{it}"):
                forward(m(e))

            @pl.when((e == nb) & used(rim))
            def _():
                with scope(f"rimb{it}"):
                    back(it, rim, True)

            @pl.when((i == 2) & used(rim))
            def _():
                with scope(f"rimfin{it}"):
                    rim_finish(it, rim)

            @pl.when(i == 2)
            def _():
                with scope(f"back{it}"):
                    back(it, order[0])

        with scope(f"tail{it}"):
            @pl.when(used(far))
            def _():
                back(it, far, True)
            back(it, order[1])
            with scope(f"fin{it}"):
                finish(it, order[0], False, False)
            with scope(f"zrim{it}"):
                z_rims(it)

            @pl.when(used(far))
            def _():
                rim_finish(it, far)
            back(it, order[2])
            if last:
                with scope(f"fin{it}"):
                    finish(it, order[1], False, False)
            with scope(f"zrs{it}"):
                z_rims_send(it)
            if not last:
                with scope(f"fin{it}"):
                    finish(it, order[1], True, False)
            for n in range(3, nb):
                back(it, order[n])
            if last:
                for n in range(2, nb):
                    with scope(f"fin{it}"):
                        finish(it, order[n], n >= nb - 2, False)
                with scope(f"zrt{it}"):
                    z_rims_take(it, order, raw)
            else:
                with scope(f"zrt{it}"):
                    z_rims_take(it, order, raw)
                for n in range(2, nb):
                    with scope(f"fin{it}"):
                        finish(it, order[n], n == nb - 1, True)

        if last:
            for n in range(nb):
                with scope("final"):
                    e = order[n]
                    if n == 0:
                        landed(zr.at[it, 0, :raw], sid["zx"] + it, to_b)
                    landed(r2.at[it, e, 0], sid["r2"] + it * ne + e, to_b)
                    for p, fresh in corrected(it, e, 0, n, raw):
                        out[p, pl.ds(pl.multiple_of((e - 1) * hw, hw), hw), :] = fresh
            with scope("sentx"):
                sends_done()


def per_device(ny, nz, estimate, view_data, block_scales, block_flags, profile, supports):
    views, planes, rows_y, rows_z = view_data.shape
    own = estimate.shape[0]
    hw = (profile.shape[2] - 1) // 2
    nb = rows_y // hw
    ne = nb + 2
    blk = planes * hw
    wide = rows_z + LANES
    tap_rows = -(-3 * views // 8) * 8
    owners = planes // own
    _, n_sem = sem_bases(ne)
    n = ITERS
    vm = pltpu.VMEM
    table = jnp.transpose(profile, (1, 0, 2))
    scratch = [
        pltpu.SMEM(block_scales.shape, F32),
        pltpu.SMEM(block_flags.shape, jnp.int32),
        vm(table.shape, F32),
        pltpu.SMEM(supports.shape, jnp.int32),
        vm((2, tap_rows, LANES), F32),
        vm((n, ne, planes, hw, rows_z), F32),
        vm((ne * blk, wide), BF),
        vm((views * blk, 3 * blk), BF),
        vm((views, blk, 3 * blk), BF),
        vm((views, rows_z, wide), BF),
        vm((views, (nb + 4) * blk, rows_z), BF),
        vm((views, (nb + 4) * blk, 2 * LANES), BF),
        vm((n, ne, planes, hw, rows_z), F32),
        vm((n, ne, 2, own, hw, rows_z), F32),
        vm((n, ne, 2, own, hw, rows_z), F32),
        vm((n, ne, 2, own, hw, rows_z), F32),
        vm((n, 2, 2, own, hw, rows_z), F32),
        vm((n, 2, ne, hw, LANES), F32),
        vm((n, 2, ne, hw, LANES), F32),
        vm((n, 2, 2, ne, hw, LANES), F32),
        vm((owners, hw, LANES), F32),
        vm((n, owners, ne, hw, LANES), F32),
        vm((n, 2, ne, hw, LANES), F32),
        vm((n, 2, ne, hw, LANES), F32),
        vm((n, 2, ne, hw, LANES), F32),
        vm((n, 2, ne, hw, LANES), F32),
        vm((n, 2, nb, hw, LANES), F32),
        vm((n, 2, nb, hw, LANES), F32),
        vm(view_data.shape, view_data.dtype),
        vm((2 * n * ne * planes * rows_z // LANES, hw, LANES), F32),
        pltpu.SemaphoreType.DMA((5 + nb,)),
        pltpu.SemaphoreType.DMA((9,)),
        pltpu.SemaphoreType.DMA((n_sem,)),
    ]
    in_hbm = pl.BlockSpec(memory_space=pltpu.HBM)
    return pl.pallas_call(
        functools.partial(kernel, (ny, nz, views, planes, rows_y, rows_z, own, hw)),
        out_shape=jax.ShapeDtypeStruct(estimate.shape, F32),
        in_specs=[in_hbm] * 6,
        out_specs=pl.BlockSpec(memory_space=pltpu.VMEM),
        scratch_shapes=scratch,
        compiler_params=pltpu.CompilerParams(
            collective_id=0, has_side_effects=True, vmem_limit_bytes=62 * 1024 * 1024
        ),
    )(estimate, view_data, block_scales, block_flags, table, supports)


def solution(mesh):
    placed = (
        P("view", "gy", "gz"),
        P("view", None, "gy", "gz"),
        P("view", "gy", "gz"),
        P("view", "gy", "gz"),
        P("view", None, None),
        P("view", None),
    )
    body = functools.partial(per_device, mesh.shape["gy"], mesh.shape["gz"])
    return jax.shard_map(
        body, mesh=mesh, in_specs=placed, out_specs=P("view", "gy", "gz"), check_vma=False
    )
```

```python
import contextlib
import functools

import jax
import jax.numpy as jnp
from jax import lax
from jax.experimental import pallas as pl
from jax.experimental.pallas import tpu as pltpu
from jax.sharding import PartitionSpec as P

BY = 32
BZ = 64
ITERS = 2
LANES = 128
MESH = pl.DeviceIdType.MESH
BF = jnp.bfloat16
F32 = jnp.float32


def scope(name):
    return contextlib.nullcontext()


def lane_iota(rows):
    return lax.broadcasted_iota(jnp.int32, (rows, LANES), 1)


def toeplitz(row, rows, shift):
    wide = jnp.broadcast_to(row, (rows, LANES))
    return pltpu.roll(wide, shift % LANES, 1, stride=1, stride_axis=0)


def roll_lanes(x, shift):
    shift = shift % LANES
    return pltpu.roll(x, shift, x.ndim - 1) if shift else x


def build_taps(dst, profile, supports, views):
    taps = profile.shape[2]
    dst[...] = jnp.zeros_like(dst)
    for vv in range(views):
        for a in range(3):
            r = 3 * vv + a
            dst[0, r : r + 1, :taps] = profile[a, vv : vv + 1, :]
    rows = dst.shape[1]
    row = lax.broadcasted_iota(jnp.int32, (rows, LANES), 0)
    lane = lane_iota(rows)
    reach = jnp.zeros((rows, LANES), jnp.int32)
    for vv in range(views):
        for a in range(3):
            reach = jnp.where(row == 3 * vv + a, supports[vv, a], reach)
    inside = (jnp.abs(lane - (taps - 1) // 2) <= reach) & (row < 3 * views)
    masked = jnp.where(inside, dst[0], 0.0)
    total = jnp.sum(masked, axis=1, keepdims=True)
    table = masked / jnp.where(total > 0.0, total, 1.0)
    turn = lax.broadcasted_iota(jnp.int32, (LANES, LANES), 0) + lax.broadcasted_iota(
        jnp.int32, (LANES, LANES), 1
    )
    flip = (turn == taps - 1).astype(F32)
    dst[0] = table
    dst[1] = jnp.dot(table, flip, precision=lax.Precision.HIGHEST, preferred_element_type=F32)


def build_plane_row(dst, row_base, kx, ky, planes, hw):
    lane = lane_iota(hw)
    per_tile = LANES // hw
    halves = planes // per_tile
    tall = toeplitz(ky, hw, 0)
    bands = []
    for d in range(3):
        q = jnp.where(lane < hw, roll_lanes(tall, -hw * d), 0.0)
        width = hw
        while width < LANES:
            q = q + roll_lanes(q, width)
            width *= 2
        bands.append(q)
    tx = toeplitz(kx, planes, -hw)
    row_id = lax.broadcasted_iota(jnp.int32, (LANES, LANES), 0)
    group = lax.broadcasted_iota(jnp.int32, (LANES, LANES), 1) // hw
    for half in range(halves):
        pick = (row_id == group + half * per_tile).astype(F32)
        spread = jnp.dot(tx, pick, precision=lax.Precision.HIGHEST, preferred_element_type=F32)
        for d in range(3):
            for x in range(planes):
                tile = spread[x : x + 1, :] * bands[d]
                c0 = (halves * d + half) * LANES
                dst[row_base + x * hw : row_base + (x + 1) * hw, c0 : c0 + LANES] = tile.astype(BF)


def build_depth(dst, v, kz, rows_z, hw):
    row_j = lax.broadcasted_iota(jnp.int32, (rows_z, LANES), 0)
    lane = lane_iota(rows_z)
    reps = rows_z // LANES
    t = jnp.concatenate([toeplitz(kz, LANES, -hw)] * reps, axis=0)
    for ct in range(reps):
        c = lane + ct * LANES
        keep = jnp.abs(c - row_j) <= hw
        dst[v, :, ct * LANES : (ct + 1) * LANES] = jnp.where(keep, t, 0.0).astype(BF)
    h = jnp.concatenate([toeplitz(kz, LANES, 0)] * reps, axis=0)
    low = (row_j < hw) & (lane < hw)
    high = (row_j >= rows_z - hw) & (lane >= hw) & (lane < 2 * hw)
    h = jnp.where(low, h, 0.0) + roll_lanes(jnp.where(high, h, 0.0), LANES // 2 - hw)
    width = hw
    while width < LANES // 2:
        h = h + roll_lanes(h, width)
        width *= 2
    dst[v, :, rows_z : rows_z + LANES] = h.astype(BF)


def sem_bases(ne):
    names = [
        ("x", ne), ("core", ne), ("y", 2), ("z", 2 * ne), ("r1", ne), ("r1z", 1), ("zb", 6),
        ("yb", 2), ("r2", ITERS * ne), ("zx", ITERS),
    ]
    bases, count = {}, 0
    for name, size in names:
        bases[name] = count
        count += size
    return bases, count


def kernel(
    sizes, est, vd_any, scales_any, flags_any, profile_any, supports_any, out,
    scales, flags, profile, supports, taps,
    fg, fb, am, bm, mt, gp, gh, ob, r1, tt, r2, yi, et, wk, wi, pk, zp, r1z, zo, zi, zt, zx, zr, vd, count,
    lsem, ssem, rsem,
):
    ny, nz, views, planes, rows_y, rows_z, own, hw = sizes
    nb = rows_y // hw
    ne = nb + 2
    blk = planes * hw
    half = LANES // 2
    v = lax.axis_index("view")
    gy = lax.axis_index("gy")
    gz = lax.axis_index("gz")
    va, vb, vc = (lax.bitwise_xor(v, 1), lax.bitwise_xor(v, 2), lax.bitwise_xor(v, 3))
    has_up, has_dn = (gy > 0, gy < ny - 1)
    has_lf, has_rt = (gz > 0, gz < nz - 1)
    yup, ydn = (jnp.maximum(gy - 1, 0), jnp.minimum(gy + 1, ny - 1))
    zlf, zrt = (jnp.maximum(gz - 1, 0), jnp.minimum(gz + 1, nz - 1))
    to_a, to_b = ({"view": va}, {"view": vb})
    to_up, to_dn = ({"gy": yup}, {"gy": ydn})
    to_lf, to_rt = ({"gz": zlf}, {"gz": zrt})
    z_dev = [[to_lf, {"gz": zlf, "view": va}], [to_rt, {"gz": zrt, "view": va}]]
    z_has = [has_lf, has_rt]
    y_has = [has_up, has_dn]
    y_to = [to_up, to_dn]
    y_co = [yup, ydn]
    z_co = [zlf, zrt]
    view_total = views * 4
    pair = (v, vb)
    other = (va, vc)
    sid, _ = sem_bases(ne)

    def mine(o):
        return pl.ds(o * own, own)

    def rcopy(src, dst, s, group, dev):
        return pltpu.make_async_remote_copy(
            src_ref=src, dst_ref=dst, send_sem=ssem.at[group], recv_sem=rsem.at[s],
            device_id=dev, device_id_type=MESH,
        )

    def landed(dst, s, dev):
        rcopy(dst, dst, s, 0, dev).wait_recv()

    def y_group(u):
        return 1 + u

    def z_group(d):
        return 3 + d

    def diag_group(d, u):
        return 5 + 2 * d + u

    def flipped(e):
        return jnp.where(has_dn, e, nb + 1 - e)

    def used(e):
        return ((e > 0) | has_up) & ((e < nb + 1) | has_dn)

    est_load = [
        pltpu.make_async_copy(
            est.at[:, b * hw : (b + 1) * hw, :], fg.at[0, b + 1, mine(v)], lsem.at[5 + b]
        )
        for b in range(nb)
    ]
    small = [
        pltpu.make_async_copy(s, d, lsem.at[i])
        for i, (s, d) in enumerate((
            (profile_any, profile), (supports_any, supports), (scales_any, scales), (flags_any, flags),
        ))
    ]
    load = pltpu.make_async_copy(vd_any, vd, lsem.at[4])
    for c in est_load:
        c.start()
    for c in small:
        c.start()
    load.start()

    barrier = pltpu.get_barrier_semaphore()
    meets = [(None, to_a), (None, to_b), (has_up, to_up), (has_dn, to_dn)]
    for d in range(2):
        for c in range(2):
            meets.append((z_has[d], z_dev[d][c]))
            for u in range(2):
                dev = dict(z_dev[d][c], gy=y_co[u])
                meets.append((z_has[d] & y_has[u], dev))
    expected = jnp.int32(0)
    for cond, dev in meets:
        if cond is None:
            pl.semaphore_signal(barrier, inc=1, device_id=dev, device_id_type=MESH)
            expected = expected + 1
        else:
            @pl.when(cond)
            def _():
                pl.semaphore_signal(barrier, inc=1, device_id=dev, device_id_type=MESH)
            expected = expected + cond.astype(jnp.int32)

    for d in range(2):
        @pl.when(jnp.logical_not(z_has[d]))
        def _():
            for it in range(ITERS):
                for c in range(2):
                    wi[it, d, c] = jnp.zeros((ne, hw, LANES), F32)
                zi[it, d] = jnp.zeros((ne, hw, LANES), F32)

        for u, e in ((0, 0), (1, nb + 1)):
            @pl.when(z_has[d] & jnp.logical_not(y_has[u]))
            def _():
                for it in range(ITERS):
                    zi[it, d, e] = jnp.zeros((hw, LANES), F32)

    for c in est_load:
        c.wait()

    def core_send(it, e, k, group=0):
        ref = fg.at[it, e, mine(pair[k])]
        rcopy(ref, ref, sid["core"] + e, group, to_a).start()

    def y_send(it, e, ks):
        for u, e_from, e_to in ((0, 1, nb + 1), (1, nb, 0)):
            @pl.when(y_has[u] & (e == e_from))
            def _():
                for k in ks:
                    rcopy(
                        fg.at[it, e_from, mine(pair[k])], fg.at[it, e_to, mine(pair[k])],
                        sid["y"] + 1 - u, y_group(u), y_to[u],
                    ).start()

    def x_send(e):
        ref = fg.at[0, e, mine(v)]
        rcopy(ref, ref, sid["x"] + e, 0, to_b).start()

    lane_h = lane_iota(hw)
    group_h = lane_h // hw
    main = slice(1, nb + 1)

    def edges(it, e, k):
        tile = jnp.zeros((hw, LANES), F32)
        for p in range(own):
            body = fg[it, e, own * pair[k] + p]
            tile = jnp.where(group_h == p, roll_lanes(body[:, :LANES], hw * p), tile)
            tile = jnp.where(
                group_h == own + p, roll_lanes(body[:, rows_z - LANES :], hw * (own + p + 1)), tile
            )
        et[it, k, e] = tile

    def by_side(near, far):
        return (
            jnp.where(lane_h < half, near, roll_lanes(far, half)),
            jnp.where(lane_h < half, roll_lanes(near, half), far),
        )

    def z_sid(side, e):
        return sid["z"] + side * ne + e

    def z_send(it, e):
        for d in range(2):
            for c in range(2):
                @pl.when(z_has[d])
                def _():
                    rcopy(wk.at[it, d, e], wi.at[it, 1 - d, c, e], z_sid(1 - d, e), z_group(d), z_dev[d][c]).start()

    def diag_send(it, e):
        for u, e_from, e_to in ((0, 1, nb + 1), (1, nb, 0)):
            for d in range(2):
                @pl.when(z_has[d] & y_has[u] & (e == e_from))
                def _():
                    for c in range(2):
                        rcopy(
                            wk.at[it, d, e_from], wi.at[it, 1 - d, c, e_to], z_sid(1 - d, e_to),
                            diag_group(d, u), dict(z_dev[d][c], gy=y_co[u]),
                        ).start()

    def z_split(it, e):
        wk[it, 0, e], wk[it, 1, e] = by_side(et[it, 0, e], et[it, 1, e])

    def gather(it, e):
        landed(fg.at[it, e, pl.ds(0, 2 * own)], sid["core"] + e, to_a)
        fb[pl.ds(pl.multiple_of(e * blk, blk), blk), :rows_z] = fg[it, e].reshape(blk, rows_z).astype(BF)

    def z_landed(it, e, cond_y=None):
        for side in range(2):
            cond = z_has[side] if cond_y is None else z_has[side] & cond_y
            @pl.when(cond)
            def _():
                landed(wi.at[it, side, :, e], z_sid(side, e), z_dev[side][0])

    def halo(it, e):
        for c in range(2):
            owners = pair if c == 0 else other
            pk[owners[0]], pk[owners[1]] = by_side(wi[it, 0, c, e], wi[it, 1, c, e])
        base = pl.multiple_of(e * blk, blk)
        for x in range(planes):
            rim = jnp.where(group_h % own == x % own, pk[x // own], 0.0)
            fb[pl.ds(base + x * hw, hw), rows_z:] = rim.astype(BF)

    def rim_forward(it):
        for u, e in ((0, 0), (1, nb + 1)):
            @pl.when(y_has[u])
            def _():
                landed(fg.at[it, e, pl.ds(0, 2 * own)], sid["y"] + u, y_to[u])
                for k in range(2):
                    core_send(it, e, k, y_group(u))

    def rim_gather(it, e):
        @pl.when(used(e))
        def _():
            gather(it, e)
            z_landed(it, e, used(e))
            halo(it, e)

    def forward(e):
        b = e - 1
        base = pl.multiple_of(b * blk, blk)
        g = jnp.dot(am[...], fb[pl.ds(base, 3 * blk), :], preferred_element_type=F32).astype(BF)
        z_block = lax.broadcasted_iota(jnp.int32, (1, rows_z), 1) // BZ
        y_block = b * hw // BY
        for vv in range(views):
            scale = jnp.zeros((1, rows_z), F32)
            valid = jnp.zeros((1, rows_z), jnp.int32)
            for c in range(rows_z // BZ):
                scale = jnp.where(z_block == c, scales[vv, y_block, c], scale)
                valid = jnp.where(z_block == c, flags[vv, y_block, c], valid)
            blurred = lax.dot_general(
                g[vv * blk : (vv + 1) * blk], mt[vv], (((1,), (1,)), ((), ())),
                preferred_element_type=F32,
            )
            data = vd[vv, :, pl.ds(pl.multiple_of(b * hw, hw), hw), :].astype(F32)
            ratio = jnp.where(
                valid == 1, data.reshape(blk, rows_z) * (scale * gains[vv][0]) / blurred, 1.0
            )
            spread = jnp.dot((ratio * gains[vv][1]).astype(BF), mt[vv], preferred_element_type=F32)
            spread = spread.astype(BF)
            gp[vv, pl.ds(base + 2 * blk, blk), :] = spread[:, :rows_z]
            gh[vv, pl.ds(base + 2 * blk, blk), :LANES] = spread[:, rows_z:]
            gh[vv, pl.ds(base + blk, blk), LANES:] = spread[:, rows_z:]

    def r1_send(it, e, group=0):
        for k in range(2):
            rcopy(ob.at[it, e, mine(other[k])], r1.at[it, e, k], sid["r1"] + e, group, to_a).start()

    def back(it, e, rim=False):
        rows = pl.ds(pl.multiple_of(e * blk, blk), 3 * blk)
        total = jnp.dot(bm[0], gp[0, rows, :], preferred_element_type=F32)
        for vv in range(1, views):
            total = total + jnp.dot(bm[vv], gp[vv, rows, :], preferred_element_type=F32)
        ob[it, e] = total.reshape(planes, hw, rows_z)
        if not rim:
            r1_send(it, e)
        else:
            for u, e_rim in ((0, 0), (1, nb + 1)):
                @pl.when(e == e_rim)
                def _():
                    r1_send(it, e_rim, y_group(u))

    def z_rims(it):
        for e in range(0, ne, 2):
            rows = slice(e * blk, (e + 3) * blk)
            total = jnp.dot(bm[0], gh[0, rows, :], preferred_element_type=F32)
            for vv in range(1, views):
                total = total + jnp.dot(bm[vv], gh[vv, rows, :], preferred_element_type=F32)
            rims = total.reshape(planes, hw, 2 * LANES)
            for n in range(2):
                for o in range(planes // own):
                    packed = rims[own * o, :, n * LANES : (n + 1) * LANES]
                    for p in range(1, own):
                        rim = rims[own * o + p, :, n * LANES : (n + 1) * LANES]
                        packed = jnp.where(group_h % own == p, rim, packed)
                    zp[it, o, e + n] = packed
        for k in range(2):
            rcopy(zp.at[it, other[k]], r1z.at[it, k], sid["r1z"], 0, to_a).start()

    zb_kinds = (
        (slice(1, nb + 1), None, slice(1, nb + 1)),
        (slice(0, 1), 0, slice(nb + 1, nb + 2)),
        (slice(nb + 1, nb + 2), 1, slice(0, 1)),
    )

    def each_zb(fn, landing=False):
        for d in range(2):
            for n, (src, u, dst) in enumerate(zb_kinds):
                u = 1 - u if landing and u is not None else u
                cond = z_has[d] if u is None else z_has[d] & y_has[u]
                dev = z_dev[d][0] if u is None else dict(z_dev[d][0], gy=y_co[u])
                @pl.when(cond)
                def _():
                    fn(d, n, src, dst, z_group(d) if u is None else diag_group(d, u), dev)

    def z_rims_send(it):
        landed(r1z.at[it], sid["r1z"], to_a)
        for e in range(ne):
            zo[it, 0, e], zo[it, 1, e] = by_side(
                zp[it, v, e] + r1z[it, 0, e], zp[it, vb, e] + r1z[it, 1, e]
            )
        each_zb(lambda d, n, src, dst, group, dev: rcopy(
            zo.at[it, d, src], zi.at[it, 1 - d, dst], sid["zb"] + 3 * (1 - d) + n, group, dev
        ).start())

    def z_rims_take(it, order, raw):
        each_zb(lambda d, n, src, dst, group, dev: landed(
            zi.at[it, d, dst], sid["zb"] + 3 * d + n, dev), True)
        for e in range(1, nb + 1):
            lf, rt = (zi[it, 0, e], zi[it, 1, e])
            if e == 1:
                lf, rt = (lf + zi[it, 0, 0], rt + zi[it, 1, 0])
            if e == nb:
                lf, rt = (lf + zi[it, 0, nb + 1], rt + zi[it, 1, nb + 1])
            zt[it, 0, e], zt[it, 1, e] = by_side(lf, rt)
        last = it + 1 == ITERS
        for n in range(raw):
            zx[it, 0, n] = zt[it, 1, order[n]]
            zx[it, 1, n] = zt[it, 0, order[n]]
        for k in range(1 if last else 2):
            rcopy(zx.at[it, k, :raw], zr.at[it, k, :raw], sid["zx"] + it, 0, to_b).start()

    def side_parts(tile, p):
        first = roll_lanes(tile, -hw * p)
        final = roll_lanes(tile, LANES - hw - half - hw * p)
        return jnp.where(lane_h < hw, first, 0.0), jnp.where(lane_h >= LANES - hw, final, 0.0)

    def rim_finish(it, e):
        landed(r1.at[it, e], sid["r1"] + e, to_a)
        for k in range(2):
            tt[it, e, k] = ob[it, e, mine(pair[k])] + r1[it, e, k]
        for u, e_from in ((0, 0), (1, nb + 1)):
            @pl.when(y_has[u] & (e == e_from))
            def _():
                rcopy(tt.at[it, e_from], yi.at[it, 1 - u], sid["yb"] + 1 - u, y_group(u), y_to[u]).start()

    def finish(it, e, edge, with_rims):
        last = it + 1 == ITERS
        landed(r1.at[it, e], sid["r1"] + e, to_a)
        if edge:
            for u, e_to in ((0, 1), (1, nb)):
                @pl.when(y_has[u] & (e == e_to))
                def _():
                    landed(yi.at[it, u], sid["yb"] + u, y_to[u])
        for k in (1, 0):
            tt[it, e, k] = ob[it, e, mine(pair[k])] + r1[it, e, k]
            if edge:
                for u, e_to in ((0, 1), (1, nb)):
                    @pl.when(y_has[u] & (e == e_to))
                    def _():
                        tt[it, e, k] = tt[it, e, k] + yi[it, u, k]
            if with_rims:
                for p in range(own):
                    first, final = side_parts(zt[it, k, e], p)
                    tt[it, e, k, p, :, :LANES] += first
                    tt[it, e, k, p, :, rows_z - LANES :] += final
            if k == 1 or not last:
                rcopy(tt.at[it, e, k], r2.at[it, e, 1 - k], sid["r2"] + it * ne + e, 0, to_b).start()

    def corrected(it, e, k, n, raw):
        tile = zt[it, k, e] + zr[it, k, n] if n < raw else None
        for p in range(own):
            total = tt[it, e, k, p] + r2[it, e, k, p]
            if tile is not None:
                first, final = side_parts(tile, p)
                total = jnp.concatenate([
                    total[:, :LANES] + first, total[:, LANES : rows_z - LANES],
                    total[:, rows_z - LANES :] + final,
                ], axis=1) if rows_z > 2 * LANES else jnp.concatenate(
                    [total[:, :LANES] + first, total[:, LANES:] + final], axis=1)
            yield p, fg[it, e, own * pair[k] + p] * total / view_total

    def m(e):
        return flipped(e)

    for e in range(1, nb + 1):
        edges(0, e, 0)
    with scope("barrier"):
        pl.semaphore_wait(barrier, expected)

    load_order = [m(e) for e in range(nb, 0, -1)]
    rcopy(et.at[0, 0, main], et.at[0, 1, main], sid["x"], 0, to_b).start()
    x_send(load_order[0])
    core_send(0, load_order[0], 0)
    y_send(0, m(nb), (0,))
    y_send(0, m(1), (0,))
    for e in load_order[1:]:
        x_send(e)
        core_send(0, e, 0)

    with scope("build"):
        for c in small:
            c.wait()
        build_taps(taps, profile, supports, views)
        for vv in range(views):
            build_depth(mt, vv, taps[0, 3 * vv + 2 : 3 * vv + 3, :], rows_z, hw)
            build_plane_row(
                am, vv * blk, taps[0, 3 * vv : 3 * vv + 1, :],
                taps[0, 3 * vv + 1 : 3 * vv + 2, :], planes, hw,
            )
        for e in (0, nb + 1):
            fb[e * blk : (e + 1) * blk, :] = jnp.zeros((blk, rows_z + LANES), BF)
    gains = []

    def build_backward():
        for vv in range(views):
            build_plane_row(
                bm.at[vv], 0, taps[1, 3 * vv : 3 * vv + 1, :],
                taps[1, 3 * vv + 1 : 3 * vv + 2, :], planes, hw,
            )
            for e in (0, 1, nb + 2, nb + 3):
                gp[vv, e * blk : (e + 1) * blk, :] = jnp.zeros((blk, rows_z), BF)
                gh[vv, e * blk : (e + 1) * blk, :LANES] = jnp.zeros((blk, LANES), BF)
            for e in (-1, 0, nb + 1, nb + 2, nb + 3):
                if e >= 0:
                    gh[vv, e * blk : (e + 1) * blk, LANES:] = jnp.zeros((blk, LANES), BF)
        for vv in range(views):
            mid = planes // 2 * hw
            along_z = mt[vv, rows_z // 2 : rows_z // 2 + 1, :rows_z].astype(F32)
            along_z = jnp.sum(along_z, axis=1, keepdims=True)
            fwd = am[vv * blk + mid : vv * blk + mid + 1, :].astype(F32)
            bwd = bm[vv, mid : mid + 1, :].astype(F32)
            gains.append((
                jnp.sum(fwd, axis=1, keepdims=True) * along_z,
                1.0 / (jnp.sum(bwd, axis=1, keepdims=True) * along_z),
            ))

    def raw_of(it):
        return nb if it + 1 == ITERS else 2

    def load_first(e):
        landed(fg.at[0, e, mine(vb)], sid["x"] + e, to_b)
        core_send(0, e, 1)

    def step_order(it):
        mid_order = [m(nb - 1), m(nb)] + [m(e) for e in range(nb - 2, 0, -1)]
        last_order = [m(e) for e in range(nb - 1, 0, -1)] + [m(nb)]
        return last_order if it + 1 == ITERS else mid_order

    def prepare_first(i):
        if i == 0:
            with scope('p_et'):
                landed(et.at[0, 1, main], sid["x"], to_b)
            for e in range(1, nb + 1):
                z_split(0, e)
            for d in range(2):
                for c in range(2):
                    @pl.when(z_has[d])
                    def _():
                        rcopy(
                            wk.at[0, d, main], wi.at[0, 1 - d, c, main], z_sid(1 - d, 1), z_group(d), z_dev[d][c]
                        ).start()
            diag_send(0, 1)
            diag_send(0, nb)
            with scope('p_first'):
                load_first(load_order[0])
            y_send(0, load_order[0], (1,))
            with scope("p_bb"):
                build_backward()
            for n, e in enumerate(load_order[1:-1]):
                with scope("p_x"):
                    load_first(e)
                gather(0, load_order[n])
                if n == 0:
                    for side in range(2):
                        @pl.when(z_has[side])
                        def _():
                            landed(wi.at[0, side, :, main], z_sid(side, 1), z_dev[side][0])
                    for q in load_order:
                        halo(0, q)
            with scope("p_rimf"):
                rim_forward(0)
            load.wait()
            with scope("p_gather"):
                gather(0, load_order[-2])
        elif i == 1:
            load_first(load_order[-1])
            y_send(0, load_order[-1], (1,))
            rim_gather(0, m(nb + 1))
        elif i == 2:
            gather(0, load_order[-1])
        elif i == 3:
            rim_gather(0, m(0))

    def update(it, n):
        order = step_order(it - 1)
        e = order[n]
        raw = raw_of(it - 1)
        if n == 0:
            landed(zr.at[it - 1, :, :raw], sid["zx"] + it - 1, to_b)
        landed(r2.at[it - 1, e], sid["r2"] + (it - 1) * ne + e, to_b)
        for k in range(2):
            for p, fresh in corrected(it - 1, e, k, n, raw):
                fg[it, e, own * pair[k] + p] = fresh
            core_send(it, e, k)
            edges(it, e, k)
        y_send(it, e, (0, 1))
        z_split(it, e)
        z_send(it, e)
        diag_send(it, e)

    def sends_done():
        plane, tile = rows_z // LANES, 1
        block = 2 * own * plane
        total = [0] * 9
        for it in range(ITERS):
            last = it + 1 == ITERS
            raw = raw_of(it)
            total[0] += nb * block * 2 + 2 * ne + nb * block // (2 if last else 1)
            total[0] += raw * (1 if last else 2)
            total[0] += nb * block // 2 + nb if it == 0 else 0
            for u in range(2):
                total[y_group(u)] += 4 * block
            for d in range(2):
                total[z_group(d)] += 2 * nb + nb
                for u in range(2):
                    total[diag_group(d, u)] += 3
        conds = [None, *y_has, *z_has, *(z_has[d] & y_has[u] for d in range(2) for u in range(2))]
        for group, (tiles, cond) in enumerate(zip(total, conds)):
            def done():
                ref = count.at[pl.ds(0, tiles)]
                rcopy(ref, ref, 0, group, to_a).wait_send()
            if cond is None:
                done()
            else:
                pl.when(cond)(done)

    def prepare_next(it, i):
        order = step_order(it - 1)
        if i == 0:
            for n in range(nb):
                with scope("update"):
                    update(it, n)
                if n == nb - 2:
                    for q in range(n):
                        gather(it, order[q])
                        z_landed(it, order[q])
                        halo(it, order[q])
                    gather(it, order[n])
                if n == nb - 1:
                    with scope("rimf"):
                        rim_forward(it)
                    with scope("halo"):
                        z_landed(it, order[n - 1])
                        halo(it, order[n - 1])
        elif i == 1:
            rim_gather(it, m(nb + 1))
        elif i == 2:
            gather(it, order[nb - 1])
            z_landed(it, order[nb - 1])
            halo(it, order[nb - 1])
        elif i == 3:
            rim_gather(it, m(0))

    for it in range(ITERS):
        last = it + 1 == ITERS
        order = step_order(it)
        raw = raw_of(it)
        top = (nb - 1, nb)
        rim = m(nb + 1)
        far = m(0)
        with scope(f"prep{it}0"):
            prepare_first(0) if it == 0 else prepare_next(it, 0)

        @pl.loop(0, nb)
        def _(i):
            for n in range(1, 4):
                @pl.when(i == n)
                def _():
                    with scope(f"prep{it}{n}"):
                        prepare_first(n) if it == 0 else prepare_next(it, n)
            e = jnp.where(i == 0, top[0], jnp.where(i == 1, top[1], nb - i))
            with scope(f"fwd{it}"):
                forward(m(e))

            @pl.when((e == nb) & used(rim))
            def _():
                with scope(f"rimb{it}"):
                    back(it, rim, True)

            @pl.when((i == 2) & used(rim))
            def _():
                with scope(f"rimfin{it}"):
                    rim_finish(it, rim)

            @pl.when(i == 2)
            def _():
                with scope(f"back{it}"):
                    back(it, order[0])

        with scope(f"tail{it}"):
            @pl.when(used(far))
            def _():
                back(it, far, True)
            back(it, order[1])
            with scope(f"fin{it}"):
                finish(it, order[0], False, False)
            with scope(f"zrim{it}"):
                z_rims(it)

            @pl.when(used(far))
            def _():
                rim_finish(it, far)
            back(it, order[2])
            if last:
                with scope(f"fin{it}"):
                    finish(it, order[1], False, False)
            with scope(f"zrs{it}"):
                z_rims_send(it)
            if not last:
                with scope(f"fin{it}"):
                    finish(it, order[1], True, False)
            for n in range(3, nb):
                back(it, order[n])
            if last:
                for n in range(2, nb):
                    with scope(f"fin{it}"):
                        finish(it, order[n], n >= nb - 2, False)
                with scope(f"zrt{it}"):
                    z_rims_take(it, order, raw)
            else:
                with scope(f"zrt{it}"):
                    z_rims_take(it, order, raw)
                for n in range(2, nb):
                    with scope(f"fin{it}"):
                        finish(it, order[n], n == nb - 1, True)

        if last:
            for n in range(nb):
                with scope("final"):
                    e = order[n]
                    if n == 0:
                        landed(zr.at[it, 0, :raw], sid["zx"] + it, to_b)
                    landed(r2.at[it, e, 0], sid["r2"] + it * ne + e, to_b)
                    for p, fresh in corrected(it, e, 0, n, raw):
                        out[p, pl.ds(pl.multiple_of((e - 1) * hw, hw), hw), :] = fresh
            with scope("sentx"):
                sends_done()


def per_device(ny, nz, estimate, view_data, block_scales, block_flags, profile, supports):
    views, planes, rows_y, rows_z = view_data.shape
    own = estimate.shape[0]
    hw = (profile.shape[2] - 1) // 2
    nb = rows_y // hw
    ne = nb + 2
    blk = planes * hw
    wide = rows_z + LANES
    tap_rows = -(-3 * views // 8) * 8
    owners = planes // own
    _, n_sem = sem_bases(ne)
    n = ITERS
    vm = pltpu.VMEM
    table = jnp.transpose(profile, (1, 0, 2))
    scratch = [
        pltpu.SMEM(block_scales.shape, F32),
        pltpu.SMEM(block_flags.shape, jnp.int32),
        vm(table.shape, F32),
        pltpu.SMEM(supports.shape, jnp.int32),
        vm((2, tap_rows, LANES), F32),
        vm((n, ne, planes, hw, rows_z), F32),
        vm((ne * blk, wide), BF),
        vm((views * blk, 3 * blk), BF),
        vm((views, blk, 3 * blk), BF),
        vm((views, rows_z, wide), BF),
        vm((views, (nb + 4) * blk, rows_z), BF),
        vm((views, (nb + 4) * blk, 2 * LANES), BF),
        vm((n, ne, planes, hw, rows_z), F32),
        vm((n, ne, 2, own, hw, rows_z), F32),
        vm((n, ne, 2, own, hw, rows_z), F32),
        vm((n, ne, 2, own, hw, rows_z), F32),
        vm((n, 2, 2, own, hw, rows_z), F32),
        vm((n, 2, ne, hw, LANES), F32),
        vm((n, 2, ne, hw, LANES), F32),
        vm((n, 2, 2, ne, hw, LANES), F32),
        vm((owners, hw, LANES), F32),
        vm((n, owners, ne, hw, LANES), F32),
        vm((n, 2, ne, hw, LANES), F32),
        vm((n, 2, ne, hw, LANES), F32),
        vm((n, 2, ne, hw, LANES), F32),
        vm((n, 2, ne, hw, LANES), F32),
        vm((n, 2, nb, hw, LANES), F32),
        vm((n, 2, nb, hw, LANES), F32),
        vm(view_data.shape, view_data.dtype),
        vm((2 * n * ne * planes * rows_z // LANES, hw, LANES), F32),
        pltpu.SemaphoreType.DMA((5 + nb,)),
        pltpu.SemaphoreType.DMA((9,)),
        pltpu.SemaphoreType.DMA((n_sem,)),
    ]
    in_hbm = pl.BlockSpec(memory_space=pltpu.HBM)
    return pl.pallas_call(
        functools.partial(kernel, (ny, nz, views, planes, rows_y, rows_z, own, hw)),
        out_shape=jax.ShapeDtypeStruct(estimate.shape, F32),
        in_specs=[in_hbm] * 6,
        out_specs=pl.BlockSpec(memory_space=pltpu.VMEM),
        scratch_shapes=scratch,
        compiler_params=pltpu.CompilerParams(
            collective_id=0, has_side_effects=True, vmem_limit_bytes=48 * 1024 * 1024
        ),
    )(*(
        pltpu.with_memory_space_constraint(x, pltpu.HBM)
        for x in (estimate, view_data, block_scales, block_flags, table, supports)
    ))


def solution(mesh):
    placed = (
        P("view", "gy", "gz"),
        P("view", None, "gy", "gz"),
        P("view", "gy", "gz"),
        P("view", "gy", "gz"),
        P("view", None, None),
        P("view", None),
    )
    body = functools.partial(per_device, mesh.shape["gy"], mesh.shape["gz"])
    return jax.shard_map(
        body, mesh=mesh, in_specs=placed, out_specs=P("view", "gy", "gz"), check_vma=False
    )
```

```python
import contextlib
import functools

import jax
import jax.numpy as jnp
from jax import lax
from jax.experimental import pallas as pl
from jax.experimental.pallas import tpu as pltpu
from jax.sharding import PartitionSpec as P

BY = 32
BZ = 64
ITERS = 2
LANES = 128
MESH = pl.DeviceIdType.MESH
BF = jnp.bfloat16
F32 = jnp.float32


def scope(name):
    return contextlib.nullcontext()


def lane_iota(rows):
    return lax.broadcasted_iota(jnp.int32, (rows, LANES), 1)


def toeplitz(row, rows, shift):
    wide = jnp.broadcast_to(row, (rows, LANES))
    return pltpu.roll(wide, shift % LANES, 1, stride=1, stride_axis=0)


def roll_lanes(x, shift):
    shift = shift % LANES
    return pltpu.roll(x, shift, x.ndim - 1) if shift else x


def build_taps(dst, profile, supports, views):
    taps = profile.shape[2]
    dst[...] = jnp.zeros_like(dst)
    for vv in range(views):
        for a in range(3):
            r = 3 * vv + a
            dst[0, r : r + 1, :taps] = profile[a, vv : vv + 1, :]
    rows = dst.shape[1]
    row = lax.broadcasted_iota(jnp.int32, (rows, LANES), 0)
    lane = lane_iota(rows)
    reach = jnp.zeros((rows, LANES), jnp.int32)
    for vv in range(views):
        for a in range(3):
            reach = jnp.where(row == 3 * vv + a, supports[vv, a], reach)
    inside = (jnp.abs(lane - (taps - 1) // 2) <= reach) & (row < 3 * views)
    masked = jnp.where(inside, dst[0], 0.0)
    total = jnp.sum(masked, axis=1, keepdims=True)
    table = masked / jnp.where(total > 0.0, total, 1.0)
    turn = lax.broadcasted_iota(jnp.int32, (LANES, LANES), 0) + lax.broadcasted_iota(
        jnp.int32, (LANES, LANES), 1
    )
    flip = (turn == taps - 1).astype(F32)
    dst[0] = table
    dst[1] = jnp.dot(table, flip, precision=lax.Precision.HIGHEST, preferred_element_type=F32)


def build_plane_row(dst, row_base, kx, ky, planes, hw):
    lane = lane_iota(hw)
    per_tile = LANES // hw
    halves = planes // per_tile
    tall = toeplitz(ky, hw, 0)
    bands = []
    for d in range(3):
        q = jnp.where(lane < hw, roll_lanes(tall, -hw * d), 0.0)
        width = hw
        while width < LANES:
            q = q + roll_lanes(q, width)
            width *= 2
        bands.append(q)
    tx = toeplitz(kx, planes, -hw)
    row_id = lax.broadcasted_iota(jnp.int32, (LANES, LANES), 0)
    group = lax.broadcasted_iota(jnp.int32, (LANES, LANES), 1) // hw
    for half in range(halves):
        pick = (row_id == group + half * per_tile).astype(F32)
        spread = jnp.dot(tx, pick, precision=lax.Precision.HIGHEST, preferred_element_type=F32)
        for d in range(3):
            for x in range(planes):
                tile = spread[x : x + 1, :] * bands[d]
                c0 = (halves * d + half) * LANES
                dst[row_base + x * hw : row_base + (x + 1) * hw, c0 : c0 + LANES] = tile.astype(BF)


def build_depth(dst, v, kz, rows_z, hw):
    row_j = lax.broadcasted_iota(jnp.int32, (rows_z, LANES), 0)
    lane = lane_iota(rows_z)
    reps = rows_z // LANES
    t = jnp.concatenate([toeplitz(kz, LANES, -hw)] * reps, axis=0)
    for ct in range(reps):
        c = lane + ct * LANES
        keep = jnp.abs(c - row_j) <= hw
        dst[v, :, ct * LANES : (ct + 1) * LANES] = jnp.where(keep, t, 0.0).astype(BF)
    h = jnp.concatenate([toeplitz(kz, LANES, 0)] * reps, axis=0)
    low = (row_j < hw) & (lane < hw)
    high = (row_j >= rows_z - hw) & (lane >= hw) & (lane < 2 * hw)
    h = jnp.where(low, h, 0.0) + roll_lanes(jnp.where(high, h, 0.0), LANES // 2 - hw)
    width = hw
    while width < LANES // 2:
        h = h + roll_lanes(h, width)
        width *= 2
    dst[v, :, rows_z : rows_z + LANES] = h.astype(BF)


def sem_bases(ne):
    names = [
        ("x", ne), ("core", ne), ("y", 2), ("z", 2 * ne), ("r1", ne), ("r1z", 1), ("zb", 6),
        ("yb", 2), ("r2", ITERS * ne), ("zx", ITERS), ("te", 1),
    ]
    bases, count = {}, 0
    for name, size in names:
        bases[name] = count
        count += size
    return bases, count


def kernel(
    sizes, est, vd_any, scales_any, flags_any, profile_any, supports_any, out,
    scales, flags, profile, supports, taps,
    fg, fb, am, bm, mt, gp, gh, ob, r1, tt, r2, yi, et, wk, wi, pk, zp, r1z, zo, zi, zt, zx, zr, te, re, vd, count, ov,
    lsem, ssem, rsem,
):
    ny, nz, views, planes, rows_y, rows_z, own, hw = sizes
    nb = rows_y // hw
    ne = nb + 2
    blk = planes * hw
    half = LANES // 2
    v = lax.axis_index("view")
    gy = lax.axis_index("gy")
    gz = lax.axis_index("gz")
    va, vb, vc = (lax.bitwise_xor(v, 1), lax.bitwise_xor(v, 2), lax.bitwise_xor(v, 3))
    has_up, has_dn = (gy > 0, gy < ny - 1)
    has_lf, has_rt = (gz > 0, gz < nz - 1)
    yup, ydn = (jnp.maximum(gy - 1, 0), jnp.minimum(gy + 1, ny - 1))
    zlf, zrt = (jnp.maximum(gz - 1, 0), jnp.minimum(gz + 1, nz - 1))
    to_a, to_b = ({"view": va}, {"view": vb})
    to_up, to_dn = ({"gy": yup}, {"gy": ydn})
    to_lf, to_rt = ({"gz": zlf}, {"gz": zrt})
    z_dev = [[to_lf, {"gz": zlf, "view": va}], [to_rt, {"gz": zrt, "view": va}]]
    z_has = [has_lf, has_rt]
    y_has = [has_up, has_dn]
    y_to = [to_up, to_dn]
    y_co = [yup, ydn]
    z_co = [zlf, zrt]
    view_total = views * 4
    pair = (v, vb)
    other = (va, vc)
    sid, _ = sem_bases(ne)

    def mine(o):
        return pl.ds(o * own, own)

    def rcopy(src, dst, s, group, dev):
        return pltpu.make_async_remote_copy(
            src_ref=src, dst_ref=dst, send_sem=ssem.at[group], recv_sem=rsem.at[s],
            device_id=dev, device_id_type=MESH,
        )

    def landed(dst, s, dev):
        rcopy(dst, dst, s, 0, dev).wait_recv()

    def y_group(u):
        return 1 + u

    def z_group(d):
        return 3 + d

    def diag_group(d, u):
        return 5 + 2 * d + u

    def flipped(e):
        return jnp.where(has_dn, e, nb + 1 - e)

    def used(e):
        return ((e > 0) | has_up) & ((e < nb + 1) | has_dn)

    est_load = [
        pltpu.make_async_copy(
            est.at[:, b * hw : (b + 1) * hw, :], fg.at[0, b + 1, mine(v)], lsem.at[5 + b]
        )
        for b in range(nb)
    ]
    small = [
        pltpu.make_async_copy(s, d, lsem.at[i])
        for i, (s, d) in enumerate((
            (profile_any, profile), (supports_any, supports), (scales_any, scales), (flags_any, flags),
        ))
    ]
    load = pltpu.make_async_copy(vd_any, vd, lsem.at[4])
    for c in est_load:
        c.start()
    for c in small:
        c.start()
    load.start()

    barrier = pltpu.get_barrier_semaphore()
    meets = [(None, to_a), (None, to_b), (has_up, to_up), (has_dn, to_dn)]
    for d in range(2):
        for c in range(2):
            meets.append((z_has[d], z_dev[d][c]))
            for u in range(2):
                dev = dict(z_dev[d][c], gy=y_co[u])
                meets.append((z_has[d] & y_has[u], dev))
    expected = jnp.int32(0)
    for cond, dev in meets:
        if cond is None:
            pl.semaphore_signal(barrier, inc=1, device_id=dev, device_id_type=MESH)
            expected = expected + 1
        else:
            @pl.when(cond)
            def _():
                pl.semaphore_signal(barrier, inc=1, device_id=dev, device_id_type=MESH)
            expected = expected + cond.astype(jnp.int32)

    for d in range(2):
        @pl.when(jnp.logical_not(z_has[d]))
        def _():
            for it in range(ITERS):
                for c in range(2):
                    wi[it, d, c] = jnp.zeros((ne, hw, LANES), F32)
                zi[it, d] = jnp.zeros((ne, hw, LANES), F32)

        for u, e in ((0, 0), (1, nb + 1)):
            @pl.when(z_has[d] & jnp.logical_not(y_has[u]))
            def _():
                for it in range(ITERS):
                    zi[it, d, e] = jnp.zeros((hw, LANES), F32)

    for c in est_load:
        c.wait()

    def core_send(it, e, k, group=0):
        ref = fg.at[it, e, mine(pair[k])]
        rcopy(ref, ref, sid["core"] + e, group, to_a).start()

    def y_send(it, e, ks):
        for u, e_from, e_to in ((0, 1, nb + 1), (1, nb, 0)):
            @pl.when(y_has[u] & (e == e_from))
            def _():
                for k in ks:
                    rcopy(
                        fg.at[it, e_from, mine(pair[k])], fg.at[it, e_to, mine(pair[k])],
                        sid["y"] + 1 - u, y_group(u), y_to[u],
                    ).start()

    def x_send(e):
        ref = fg.at[0, e, mine(v)]
        rcopy(ref, ref, sid["x"] + e, 0, to_b).start()

    lane_h = lane_iota(hw)
    group_h = lane_h // hw
    main = slice(1, nb + 1)

    def edge_tile(bodies):
        tile = jnp.zeros((hw, LANES), F32)
        for p, body in enumerate(bodies):
            tile = jnp.where(group_h == p, roll_lanes(body[:, :LANES], hw * p), tile)
            tile = jnp.where(
                group_h == own + p, roll_lanes(body[:, rows_z - LANES :], hw * (own + p + 1)), tile
            )
        return tile

    def edges(it, e, k):
        et[it, k, e] = edge_tile([fg[it, e, own * pair[k] + p] for p in range(own)])

    def by_side(near, far):
        return (
            jnp.where(lane_h < half, near, roll_lanes(far, half)),
            jnp.where(lane_h < half, roll_lanes(near, half), far),
        )

    def z_sid(side, e):
        return sid["z"] + side * ne + e

    def z_send(it, e):
        for d in range(2):
            for c in range(2):
                @pl.when(z_has[d])
                def _():
                    rcopy(wk.at[it, d, e], wi.at[it, 1 - d, c, e], z_sid(1 - d, e), z_group(d), z_dev[d][c]).start()

    def diag_send(it, e):
        for u, e_from, e_to in ((0, 1, nb + 1), (1, nb, 0)):
            for d in range(2):
                @pl.when(z_has[d] & y_has[u] & (e == e_from))
                def _():
                    for c in range(2):
                        rcopy(
                            wk.at[it, d, e_from], wi.at[it, 1 - d, c, e_to], z_sid(1 - d, e_to),
                            diag_group(d, u), dict(z_dev[d][c], gy=y_co[u]),
                        ).start()

    def z_split(it, e):
        wk[it, 0, e], wk[it, 1, e] = by_side(et[it, 0, e], et[it, 1, e])

    def gather(it, e):
        landed(fg.at[it, e, pl.ds(0, 2 * own)], sid["core"] + e, to_a)
        fb[pl.ds(pl.multiple_of(e * blk, blk), blk), :rows_z] = fg[it, e].reshape(blk, rows_z).astype(BF)

    def z_landed(it, e, cond_y=None):
        for side in range(2):
            cond = z_has[side] if cond_y is None else z_has[side] & cond_y
            @pl.when(cond)
            def _():
                landed(wi.at[it, side, :, e], z_sid(side, e), z_dev[side][0])

    def halo(it, e):
        for c in range(2):
            owners = pair if c == 0 else other
            pk[owners[0]], pk[owners[1]] = by_side(wi[it, 0, c, e], wi[it, 1, c, e])
        base = pl.multiple_of(e * blk, blk)
        for x in range(planes):
            rim = jnp.where(group_h % own == x % own, pk[x // own], 0.0)
            fb[pl.ds(base + x * hw, hw), rows_z:] = rim.astype(BF)

    def rim_forward(it):
        for u, e in ((0, 0), (1, nb + 1)):
            @pl.when(y_has[u])
            def _():
                landed(fg.at[it, e, pl.ds(0, 2 * own)], sid["y"] + u, y_to[u])
                for k in range(2):
                    core_send(it, e, k, y_group(u))

    def rim_gather(it, e):
        @pl.when(used(e))
        def _():
            gather(it, e)
            z_landed(it, e, used(e))
            halo(it, e)

    def forward(e):
        b = e - 1
        base = pl.multiple_of(b * blk, blk)
        g = jnp.dot(am[...], fb[pl.ds(base, 3 * blk), :], preferred_element_type=F32).astype(BF)
        z_block = lax.broadcasted_iota(jnp.int32, (1, rows_z), 1) // BZ
        y_block = b * hw // BY
        for vv in range(views):
            scale = jnp.zeros((1, rows_z), F32)
            valid = jnp.zeros((1, rows_z), jnp.int32)
            for c in range(rows_z // BZ):
                scale = jnp.where(z_block == c, scales[vv, y_block, c], scale)
                valid = jnp.where(z_block == c, flags[vv, y_block, c], valid)
            blurred = lax.dot_general(
                g[vv * blk : (vv + 1) * blk], mt[vv], (((1,), (1,)), ((), ())),
                preferred_element_type=F32,
            )
            data = vd[vv, :, pl.ds(pl.multiple_of(b * hw, hw), hw), :].astype(F32)
            ratio = jnp.where(
                valid == 1, data.reshape(blk, rows_z) * (scale * gains[vv][0]) / blurred, 1.0
            )
            spread = jnp.dot((ratio * gains[vv][1]).astype(BF), mt[vv], preferred_element_type=F32)
            spread = spread.astype(BF)
            gp[vv, pl.ds(base + 2 * blk, blk), :] = spread[:, :rows_z]
            gh[vv, pl.ds(base + 2 * blk, blk), :LANES] = spread[:, rows_z:]
            gh[vv, pl.ds(base + blk, blk), LANES:] = spread[:, rows_z:]

    def r1_send(it, e, group=0):
        for k in range(2):
            rcopy(ob.at[it, e, mine(other[k])], r1.at[it, e, k], sid["r1"] + e, group, to_a).start()

    def back(it, e, rim=False):
        rows = pl.ds(pl.multiple_of(e * blk, blk), 3 * blk)
        total = jnp.dot(bm[0], gp[0, rows, :], preferred_element_type=F32)
        for vv in range(1, views):
            total = total + jnp.dot(bm[vv], gp[vv, rows, :], preferred_element_type=F32)
        ob[it, e] = total.reshape(planes, hw, rows_z)
        if not rim:
            r1_send(it, e)
        else:
            for u, e_rim in ((0, 0), (1, nb + 1)):
                @pl.when(e == e_rim)
                def _():
                    r1_send(it, e_rim, y_group(u))

    def z_pair(it, e):
        rows = pl.ds(pl.multiple_of(e * blk, blk), 3 * blk)
        total = jnp.dot(bm[0], gh[0, rows, :], preferred_element_type=F32)
        for vv in range(1, views):
            total = total + jnp.dot(bm[vv], gh[vv, rows, :], preferred_element_type=F32)
        rims = total.reshape(planes, hw, 2 * LANES)
        for n in range(2):
            for o in range(planes // own):
                packed = rims[own * o, :, n * LANES : (n + 1) * LANES]
                for p in range(1, own):
                    rim = rims[own * o + p, :, n * LANES : (n + 1) * LANES]
                    packed = jnp.where(group_h % own == p, rim, packed)
                zp[it, o, e + n] = packed

    def z_rims_sum(it):
        for k in range(2):
            rcopy(zp.at[it, other[k]], r1z.at[it, k], sid["r1z"], 0, to_a).start()

    zb_kinds = (
        (slice(1, nb + 1), None, slice(1, nb + 1)),
        (slice(0, 1), 0, slice(nb + 1, nb + 2)),
        (slice(nb + 1, nb + 2), 1, slice(0, 1)),
    )

    def each_zb(fn, landing=False):
        for d in range(2):
            for n, (src, u, dst) in enumerate(zb_kinds):
                u = 1 - u if landing and u is not None else u
                cond = z_has[d] if u is None else z_has[d] & y_has[u]
                dev = z_dev[d][0] if u is None else dict(z_dev[d][0], gy=y_co[u])
                @pl.when(cond)
                def _():
                    fn(d, n, src, dst, z_group(d) if u is None else diag_group(d, u), dev)

    def z_rims_send(it):
        landed(r1z.at[it], sid["r1z"], to_a)
        for e in range(ne):
            zo[it, 0, e], zo[it, 1, e] = by_side(
                zp[it, v, e] + r1z[it, 0, e], zp[it, vb, e] + r1z[it, 1, e]
            )
        each_zb(lambda d, n, src, dst, group, dev: rcopy(
            zo.at[it, d, src], zi.at[it, 1 - d, dst], sid["zb"] + 3 * (1 - d) + n, group, dev
        ).start())

    def z_rims_take(it, order, raw):
        each_zb(lambda d, n, src, dst, group, dev: landed(
            zi.at[it, d, dst], sid["zb"] + 3 * d + n, dev), True)
        for e in range(1, nb + 1):
            lf, rt = (zi[it, 0, e], zi[it, 1, e])
            if e == 1:
                lf, rt = (lf + zi[it, 0, 0], rt + zi[it, 1, 0])
            if e == nb:
                lf, rt = (lf + zi[it, 0, nb + 1], rt + zi[it, 1, nb + 1])
            zt[it, 0, e], zt[it, 1, e] = by_side(lf, rt)
        last = it + 1 == ITERS
        for n in range(raw):
            zx[it, 0, n] = zt[it, 1, order[n]]
            zx[it, 1, n] = zt[it, 0, order[n]]
        for k in range(1 if last else 2):
            rcopy(zx.at[it, k, :raw], zr.at[it, k, :raw], sid["zx"] + it, 0, to_b).start()

    def side_parts(tile, p):
        first = roll_lanes(tile, -hw * p)
        final = roll_lanes(tile, LANES - hw - half - hw * p)
        return jnp.where(lane_h < hw, first, 0.0), jnp.where(lane_h >= LANES - hw, final, 0.0)

    def rim_finish(it, e):
        landed(r1.at[it, e], sid["r1"] + e, to_a)
        for k in range(2):
            tt[it, e, k] = ob[it, e, mine(pair[k])] + r1[it, e, k]
        for u, e_from in ((0, 0), (1, nb + 1)):
            @pl.when(y_has[u] & (e == e_from))
            def _():
                rcopy(tt.at[it, e_from], yi.at[it, 1 - u], sid["yb"] + 1 - u, y_group(u), y_to[u]).start()

    def finish(it, e, edge, with_rims, send=True):
        landed(r1.at[it, e], sid["r1"] + e, to_a)
        if edge:
            for u, e_to in ((0, 1), (1, nb)):
                @pl.when(y_has[u] & (e == e_to))
                def _():
                    landed(yi.at[it, u], sid["yb"] + u, y_to[u])
        for k in (1, 0):
            tt[it, e, k] = ob[it, e, mine(pair[k])] + r1[it, e, k]
            if edge:
                for u, e_to in ((0, 1), (1, nb)):
                    @pl.when(y_has[u] & (e == e_to))
                    def _():
                        tt[it, e, k] = tt[it, e, k] + yi[it, u, k]
            if with_rims:
                for p in range(own):
                    first, final = side_parts(zt[it, k, e], p)
                    tt[it, e, k, p, :, :LANES] += first
                    tt[it, e, k, p, :, rows_z - LANES :] += final
        if send:
            sums_send(it, e)

    def sums_send(it, e):
        last = it + 1 == ITERS
        for k in (1,) if last else (1, 0):
            rcopy(tt.at[it, e, k], r2.at[it, e, 1 - k], sid["r2"] + it * ne + e, 0, to_b).start()

    def rest_send(it, order, raw):
        count = nb - raw
        for k in range(2):
            for n in range(count):
                te[it, 1 - k, n] = edge_tile([tt[it, order[raw + n], k, p] for p in range(own)])
        rcopy(te.at[it, :, :count], re.at[it, :, :count], sid["te"], 0, to_b).start()
        for n in range(raw, nb):
            sums_send(it, order[n])

    def rest_edges(it, order, raw):
        landed(re.at[it - 1, :, : nb - raw], sid["te"], to_b)
        for n in range(raw, nb):
            e = order[n]
            for k in range(2):
                total = te[it - 1, 1 - k, n - raw] + re[it - 1, k, n - raw]
                et[it, k, e] = et[it - 1, k, e] * total / view_total
            z_split(it, e)
            z_send(it, e)
            diag_send(it, e)

    def corrected(it, e, k, n, raw):
        tile = zt[it, k, e] + zr[it, k, n] if n < raw else None
        for p in range(own):
            total = tt[it, e, k, p] + r2[it, e, k, p]
            if tile is not None:
                first, final = side_parts(tile, p)
                total = jnp.concatenate([
                    total[:, :LANES] + first, total[:, LANES : rows_z - LANES],
                    total[:, rows_z - LANES :] + final,
                ], axis=1) if rows_z > 2 * LANES else jnp.concatenate(
                    [total[:, :LANES] + first, total[:, LANES:] + final], axis=1)
            yield p, fg[it, e, own * pair[k] + p] * total / view_total

    def m(e):
        return flipped(e)

    for e in range(1, nb + 1):
        edges(0, e, 0)
    with scope("barrier"):
        pl.semaphore_wait(barrier, expected)

    load_order = [m(e) for e in range(nb, 0, -1)]
    rcopy(et.at[0, 0, main], et.at[0, 1, main], sid["x"], 0, to_b).start()
    x_send(load_order[0])
    core_send(0, load_order[0], 0)
    y_send(0, m(nb), (0,))
    y_send(0, m(1), (0,))
    for e in load_order[1:]:
        x_send(e)
        core_send(0, e, 0)

    with scope("build"):
        for c in small:
            c.wait()
        build_taps(taps, profile, supports, views)
        for vv in range(views):
            build_depth(mt, vv, taps[0, 3 * vv + 2 : 3 * vv + 3, :], rows_z, hw)
            build_plane_row(
                am, vv * blk, taps[0, 3 * vv : 3 * vv + 1, :],
                taps[0, 3 * vv + 1 : 3 * vv + 2, :], planes, hw,
            )
        for e in (0, nb + 1):
            fb[e * blk : (e + 1) * blk, :] = jnp.zeros((blk, rows_z + LANES), BF)
    gains = []

    def build_backward():
        for vv in range(views):
            build_plane_row(
                bm.at[vv], 0, taps[1, 3 * vv : 3 * vv + 1, :],
                taps[1, 3 * vv + 1 : 3 * vv + 2, :], planes, hw,
            )
            for e in (0, 1, nb + 2, nb + 3):
                gp[vv, e * blk : (e + 1) * blk, :] = jnp.zeros((blk, rows_z), BF)
                gh[vv, e * blk : (e + 1) * blk, :LANES] = jnp.zeros((blk, LANES), BF)
            for e in (-1, 0, nb + 1, nb + 2, nb + 3):
                if e >= 0:
                    gh[vv, e * blk : (e + 1) * blk, LANES:] = jnp.zeros((blk, LANES), BF)
        for vv in range(views):
            mid = planes // 2 * hw
            along_z = mt[vv, rows_z // 2 : rows_z // 2 + 1, :rows_z].astype(F32)
            along_z = jnp.sum(along_z, axis=1, keepdims=True)
            fwd = am[vv * blk + mid : vv * blk + mid + 1, :].astype(F32)
            bwd = bm[vv, mid : mid + 1, :].astype(F32)
            gains.append((
                jnp.sum(fwd, axis=1, keepdims=True) * along_z,
                1.0 / (jnp.sum(bwd, axis=1, keepdims=True) * along_z),
            ))

    def raw_of(it):
        return nb if it + 1 == ITERS else 2

    def load_first(e):
        landed(fg.at[0, e, mine(vb)], sid["x"] + e, to_b)
        core_send(0, e, 1)

    def step_order(it):
        mid_order = [m(nb - 1), m(nb)] + [m(e) for e in range(nb - 2, 0, -1)]
        last_order = [m(e) for e in range(nb - 1, 0, -1)] + [m(nb)]
        return last_order if it + 1 == ITERS else mid_order

    def prepare_first(i):
        if i == 0:
            with scope('p_et'):
                landed(et.at[0, 1, main], sid["x"], to_b)
            for e in range(1, nb + 1):
                z_split(0, e)
            for d in range(2):
                for c in range(2):
                    @pl.when(z_has[d])
                    def _():
                        rcopy(
                            wk.at[0, d, main], wi.at[0, 1 - d, c, main], z_sid(1 - d, 1), z_group(d), z_dev[d][c]
                        ).start()
            diag_send(0, 1)
            diag_send(0, nb)
            with scope('p_first'):
                load_first(load_order[0])
            y_send(0, load_order[0], (1,))
            with scope("p_bb"):
                build_backward()
            for n, e in enumerate(load_order[1:-1]):
                with scope("p_x"):
                    load_first(e)
                if n < nb - 3:
                    gather(0, load_order[n])
            with scope("p_z"):
                for side in range(2):
                    @pl.when(z_has[side])
                    def _():
                        landed(wi.at[0, side, :, main], z_sid(side, 1), z_dev[side][0])
                for q in load_order:
                    halo(0, q)
            gather(0, load_order[-3])
            with scope("p_rimf"):
                rim_forward(0)
            load.wait()
            with scope("p_gather"):
                gather(0, load_order[-2])
        elif i == 1:
            load_first(load_order[-1])
            y_send(0, load_order[-1], (1,))
            rim_gather(0, m(nb + 1))
        elif i == 2:
            gather(0, load_order[-1])
        elif i == 3:
            rim_gather(0, m(0))

    def update(it, n):
        order = step_order(it - 1)
        e = order[n]
        raw = raw_of(it - 1)
        if n == 0:
            landed(zr.at[it - 1, :, :raw], sid["zx"] + it - 1, to_b)
        landed(r2.at[it - 1, e], sid["r2"] + (it - 1) * ne + e, to_b)
        for k in range(2):
            for p, fresh in corrected(it - 1, e, k, n, raw):
                fg[it, e, own * pair[k] + p] = fresh
            core_send(it, e, k)
            if n < raw:
                edges(it, e, k)
        y_send(it, e, (0, 1))
        if n < raw:
            z_split(it, e)
            z_send(it, e)
            diag_send(it, e)

    def sends_done():
        plane, tile = rows_z // LANES, 1
        block = 2 * own * plane
        total = [0] * 9
        for it in range(ITERS):
            last = it + 1 == ITERS
            raw = raw_of(it)
            total[0] += nb * block * 2 + 2 * ne + nb * block // (2 if last else 1)
            total[0] += raw if last else 2 * nb
            total[0] += nb * block // 2 + nb if it == 0 else 0
            for u in range(2):
                total[y_group(u)] += 4 * block
            for d in range(2):
                total[z_group(d)] += 2 * nb + nb
                for u in range(2):
                    total[diag_group(d, u)] += 3
        conds = [None, *y_has, *z_has, *(z_has[d] & y_has[u] for d in range(2) for u in range(2))]
        for group, (tiles, cond) in enumerate(zip(total, conds)):
            def done():
                ref = count.at[pl.ds(0, tiles)]
                rcopy(ref, ref, 0, group, to_a).wait_send()
            if cond is None:
                done()
            else:
                pl.when(cond)(done)

    def prepare_next(it, i):
        order = step_order(it - 1)
        if i == 0:
            raw = raw_of(it - 1)
            for n in range(nb - 1):
                with scope(f"upd{n}"):
                    update(it, n)
                if n == raw - 1:
                    with scope("rest"):
                        rest_edges(it, order, raw)
                    for q in range(n):
                        gather(it, order[q])
                        z_landed(it, order[q])
                        halo(it, order[q])
            with scope("gath"):
                for q in range(raw - 1, nb - 1):
                    z_landed(it, order[q])
                    halo(it, order[q])
                    gather(it, order[q])
                z_landed(it, order[nb - 1])
                halo(it, order[nb - 1])
        elif i == 1:
            with scope("rimf"):
                rim_forward(it)
            with scope("upd3"):
                update(it, nb - 1)
            with scope("rimg"):
                rim_gather(it, m(nb + 1))
        elif i == 2:
            with scope("gath"):
                gather(it, order[nb - 1])
        elif i == 3:
            rim_gather(it, m(0))

    def out_copy(n, e):
        rows = pl.ds(pl.multiple_of((e - 1) * hw, hw), hw)
        return pltpu.make_async_copy(ov.at[e], out.at[:, rows, :], lsem.at[5 + n])

    for it in range(ITERS):
        last = it + 1 == ITERS
        order = step_order(it)
        raw = raw_of(it)
        top = (nb - 1, nb)
        rim = m(nb + 1)
        far = m(0)
        near = jnp.where(has_dn, nb, 0)
        with scope(f"prep{it}0"):
            prepare_first(0) if it == 0 else prepare_next(it, 0)

        @pl.loop(0, nb)
        def _(i):
            for n in range(1, 4):
                @pl.when(i == n)
                def _():
                    with scope(f"prep{it}{n}"):
                        prepare_first(n) if it == 0 else prepare_next(it, n)
            e = jnp.where(i == 0, top[0], jnp.where(i == 1, top[1], nb - i))
            with scope(f"fwd{it}"):
                forward(m(e))

            @pl.when((e == nb) & used(rim))
            def _():
                with scope(f"rimb{it}"):
                    back(it, rim, True)

            @pl.when((i == 2) & used(rim))
            def _():
                with scope(f"rimfin{it}"):
                    rim_finish(it, rim)

            @pl.when(i == 2)
            def _():
                with scope(f"back{it}"):
                    back(it, order[0])

        with scope(f"tail{it}"):
            @pl.when(used(far))
            def _():
                back(it, far, True)
            with scope(f"fin{it}"):
                finish(it, order[0], False, False)
            if last:
                back(it, order[1])
            with scope(f"zrim{it}"):
                for e in range(0, ne, 2):
                    z_pair(it, e)
            z_rims_sum(it)
            if not last:
                back(it, order[1])

            @pl.when(used(far))
            def _():
                rim_finish(it, far)
            back(it, order[2])
            if last:
                with scope(f"fin{it}"):
                    finish(it, order[1], False, False)
            with scope(f"zrs{it}"):
                z_rims_send(it)
            if not last:
                with scope(f"fin{it}"):
                    finish(it, order[1], True, False)
            for n in range(3, nb):
                back(it, order[n])
            if last:
                for n in range(2, nb):
                    with scope(f"fin{it}"):
                        finish(it, order[n], n >= nb - 2, False)
                with scope(f"zrt{it}"):
                    z_rims_take(it, order, raw)
            else:
                with scope(f"zrt{it}"):
                    z_rims_take(it, order, raw)
                for n in range(2, nb):
                    with scope(f"fin{it}"):
                        finish(it, order[n], n == nb - 1, True, False)
                with scope(f"rests{it}"):
                    rest_send(it, order, raw)

        if last:
            for n in range(nb):
                with scope("final"):
                    e = order[n]
                    if n == 0:
                        landed(zr.at[it, 0, :raw], sid["zx"] + it, to_b)
                    landed(r2.at[it, e, 0], sid["r2"] + it * ne + e, to_b)
                    for p, fresh in corrected(it, e, 0, n, raw):
                        ov[e, p] = fresh
                    out_copy(n, e).start()
            for n in range(nb):
                out_copy(n, order[n]).wait()
            with scope("sentx"):
                sends_done()


def per_device(ny, nz, estimate, view_data, block_scales, block_flags, profile, supports):
    views, planes, rows_y, rows_z = view_data.shape
    own = estimate.shape[0]
    hw = (profile.shape[2] - 1) // 2
    nb = rows_y // hw
    ne = nb + 2
    blk = planes * hw
    wide = rows_z + LANES
    tap_rows = -(-3 * views // 8) * 8
    owners = planes // own
    _, n_sem = sem_bases(ne)
    n = ITERS
    vm = pltpu.VMEM
    table = jnp.transpose(profile, (1, 0, 2))
    scratch = [
        pltpu.SMEM(block_scales.shape, F32),
        pltpu.SMEM(block_flags.shape, jnp.int32),
        vm(table.shape, F32),
        pltpu.SMEM(supports.shape, jnp.int32),
        vm((2, tap_rows, LANES), F32),
        vm((n, ne, planes, hw, rows_z), F32),
        vm((ne * blk, wide), BF),
        vm((views * blk, 3 * blk), BF),
        vm((views, blk, 3 * blk), BF),
        vm((views, rows_z, wide), BF),
        vm((views, (nb + 4) * blk, rows_z), BF),
        vm((views, (nb + 4) * blk, 2 * LANES), BF),
        vm((n, ne, planes, hw, rows_z), F32),
        vm((n, ne, 2, own, hw, rows_z), F32),
        vm((n, ne, 2, own, hw, rows_z), F32),
        vm((n, ne, 2, own, hw, rows_z), F32),
        vm((n, 2, 2, own, hw, rows_z), F32),
        vm((n, 2, ne, hw, LANES), F32),
        vm((n, 2, ne, hw, LANES), F32),
        vm((n, 2, 2, ne, hw, LANES), F32),
        vm((owners, hw, LANES), F32),
        vm((n, owners, ne, hw, LANES), F32),
        vm((n, 2, ne, hw, LANES), F32),
        vm((n, 2, ne, hw, LANES), F32),
        vm((n, 2, ne, hw, LANES), F32),
        vm((n, 2, ne, hw, LANES), F32),
        vm((n, 2, nb, hw, LANES), F32),
        vm((n, 2, nb, hw, LANES), F32),
        vm((n, 2, nb, hw, LANES), F32),
        vm((n, 2, nb, hw, LANES), F32),
        vm(view_data.shape, view_data.dtype),
        vm((2 * n * ne * planes * rows_z // LANES, hw, LANES), F32),
        vm((ne, own, hw, rows_z), F32),
        pltpu.SemaphoreType.DMA((5 + nb,)),
        pltpu.SemaphoreType.DMA((9,)),
        pltpu.SemaphoreType.DMA((n_sem,)),
    ]
    in_hbm = pl.BlockSpec(memory_space=pltpu.HBM)
    return pl.pallas_call(
        functools.partial(kernel, (ny, nz, views, planes, rows_y, rows_z, own, hw)),
        out_shape=jax.ShapeDtypeStruct(estimate.shape, F32),
        in_specs=[in_hbm] * 6,
        out_specs=pl.BlockSpec(memory_space=pl.ANY),
        scratch_shapes=scratch,
        compiler_params=pltpu.CompilerParams(
            collective_id=0, has_side_effects=True, vmem_limit_bytes=48 * 1024 * 1024
        ),
    )(*(
        pltpu.with_memory_space_constraint(x, pltpu.HBM)
        for x in (estimate, view_data, block_scales, block_flags, table, supports)
    ))


def solution(mesh):
    placed = (
        P("view", "gy", "gz"),
        P("view", None, "gy", "gz"),
        P("view", "gy", "gz"),
        P("view", "gy", "gz"),
        P("view", None, None),
        P("view", None),
    )
    body = functools.partial(per_device, mesh.shape["gy"], mesh.shape["gz"])
    return jax.shard_map(
        body, mesh=mesh, in_specs=placed, out_specs=P("view", "gy", "gz"), check_vma=False
    )
```

```python
import contextlib
import functools

import jax
import jax.numpy as jnp
from jax import lax
from jax.experimental import pallas as pl
from jax.experimental.pallas import tpu as pltpu
from jax.sharding import PartitionSpec as P

BY = 32
BZ = 64
ITERS = 2
LANES = 128
MESH = pl.DeviceIdType.MESH
BF = jnp.bfloat16
F32 = jnp.float32


def scope(name):
    return contextlib.nullcontext()


def lane_iota(rows):
    return lax.broadcasted_iota(jnp.int32, (rows, LANES), 1)


def toeplitz(row, rows, shift):
    wide = jnp.broadcast_to(row, (rows, LANES))
    return pltpu.roll(wide, shift % LANES, 1, stride=1, stride_axis=0)


def roll_lanes(x, shift):
    shift = shift % LANES
    return pltpu.roll(x, shift, x.ndim - 1) if shift else x


def build_taps(dst, profile, supports, views):
    taps = profile.shape[2]
    dst[...] = jnp.zeros_like(dst)
    for vv in range(views):
        for a in range(3):
            r = 3 * vv + a
            dst[0, r : r + 1, :taps] = profile[a, vv : vv + 1, :]
    rows = dst.shape[1]
    row = lax.broadcasted_iota(jnp.int32, (rows, LANES), 0)
    lane = lane_iota(rows)
    reach = jnp.zeros((rows, LANES), jnp.int32)
    for vv in range(views):
        for a in range(3):
            reach = jnp.where(row == 3 * vv + a, supports[vv, a], reach)
    inside = (jnp.abs(lane - (taps - 1) // 2) <= reach) & (row < 3 * views)
    masked = jnp.where(inside, dst[0], 0.0)
    total = jnp.sum(masked, axis=1, keepdims=True)
    table = masked / jnp.where(total > 0.0, total, 1.0)
    turn = lax.broadcasted_iota(jnp.int32, (LANES, LANES), 0) + lax.broadcasted_iota(
        jnp.int32, (LANES, LANES), 1
    )
    flip = (turn == taps - 1).astype(F32)
    dst[0] = table
    dst[1] = jnp.dot(table, flip, precision=lax.Precision.HIGHEST, preferred_element_type=F32)


def build_plane_row(dst, row_base, kx, ky, planes, hw):
    lane = lane_iota(hw)
    per_tile = LANES // hw
    halves = planes // per_tile
    tall = toeplitz(ky, hw, 0)
    bands = []
    for d in range(3):
        q = jnp.where(lane < hw, roll_lanes(tall, -hw * d), 0.0)
        width = hw
        while width < LANES:
            q = q + roll_lanes(q, width)
            width *= 2
        bands.append(q)
    tx = toeplitz(kx, planes, -hw)
    row_id = lax.broadcasted_iota(jnp.int32, (LANES, LANES), 0)
    group = lax.broadcasted_iota(jnp.int32, (LANES, LANES), 1) // hw
    for half in range(halves):
        pick = (row_id == group + half * per_tile).astype(F32)
        spread = jnp.dot(tx, pick, precision=lax.Precision.HIGHEST, preferred_element_type=F32)
        for d in range(3):
            for x in range(planes):
                tile = spread[x : x + 1, :] * bands[d]
                c0 = (halves * d + half) * LANES
                dst[row_base + x * hw : row_base + (x + 1) * hw, c0 : c0 + LANES] = tile.astype(BF)


def build_depth(dst, v, kz, rows_z, hw):
    row_j = lax.broadcasted_iota(jnp.int32, (rows_z, LANES), 0)
    lane = lane_iota(rows_z)
    reps = rows_z // LANES
    t = jnp.concatenate([toeplitz(kz, LANES, -hw)] * reps, axis=0)
    for ct in range(reps):
        c = lane + ct * LANES
        keep = jnp.abs(c - row_j) <= hw
        dst[v, :, ct * LANES : (ct + 1) * LANES] = jnp.where(keep, t, 0.0).astype(BF)
    h = jnp.concatenate([toeplitz(kz, LANES, 0)] * reps, axis=0)
    low = (row_j < hw) & (lane < hw)
    high = (row_j >= rows_z - hw) & (lane >= hw) & (lane < 2 * hw)
    h = jnp.where(low, h, 0.0) + roll_lanes(jnp.where(high, h, 0.0), LANES // 2 - hw)
    width = hw
    while width < LANES // 2:
        h = h + roll_lanes(h, width)
        width *= 2
    dst[v, :, rows_z : rows_z + LANES] = h.astype(BF)


def sem_bases(ne):
    names = [
        ("x", ne), ("core", ne), ("y", 2), ("z", 2 * ne), ("r1", ne), ("r1z", 1), ("zb", 6),
        ("yb", 2), ("r2", ITERS * ne), ("zx", ITERS), ("te", 1),
    ]
    bases, count = {}, 0
    for name, size in names:
        bases[name] = count
        count += size
    return bases, count


def kernel(
    sizes, est, vd_any, scales_any, flags_any, profile_any, supports_any, out,
    scales, flags, profile, supports, taps,
    fg, fb, am, bm, mt, gp, gh, ob, r1, tt, r2, yi, et, wk, wi, pk, zp, r1z, zo, zi, zt, zx, zr, te, re, vd, count, ov,
    lsem, ssem, rsem,
):
    ny, nz, views, planes, rows_y, rows_z, own, hw = sizes
    nb = rows_y // hw
    ne = nb + 2
    blk = planes * hw
    half = LANES // 2
    v = lax.axis_index("view")
    gy = lax.axis_index("gy")
    gz = lax.axis_index("gz")
    va, vb, vc = (lax.bitwise_xor(v, 1), lax.bitwise_xor(v, 2), lax.bitwise_xor(v, 3))
    has_up, has_dn = (gy > 0, gy < ny - 1)
    has_lf, has_rt = (gz > 0, gz < nz - 1)
    yup, ydn = (jnp.maximum(gy - 1, 0), jnp.minimum(gy + 1, ny - 1))
    zlf, zrt = (jnp.maximum(gz - 1, 0), jnp.minimum(gz + 1, nz - 1))
    to_a, to_b = ({"view": va}, {"view": vb})
    to_up, to_dn = ({"gy": yup}, {"gy": ydn})
    to_lf, to_rt = ({"gz": zlf}, {"gz": zrt})
    z_dev = [[to_lf, {"gz": zlf, "view": va}], [to_rt, {"gz": zrt, "view": va}]]
    z_has = [has_lf, has_rt]
    y_has = [has_up, has_dn]
    y_to = [to_up, to_dn]
    y_co = [yup, ydn]
    z_co = [zlf, zrt]
    view_total = views * 4
    pair = (v, vb)
    other = (va, vc)
    sid, _ = sem_bases(ne)

    def mine(o):
        return pl.ds(o * own, own)

    def rcopy(src, dst, s, group, dev):
        return pltpu.make_async_remote_copy(
            src_ref=src, dst_ref=dst, send_sem=ssem.at[group], recv_sem=rsem.at[s],
            device_id=dev, device_id_type=MESH,
        )

    def landed(dst, s, dev):
        rcopy(dst, dst, s, 0, dev).wait_recv()

    def y_group(u):
        return 1 + u

    def z_group(d):
        return 3 + d

    def diag_group(d, u):
        return 5 + 2 * d + u

    def flipped(e):
        return jnp.where(has_dn, e, nb + 1 - e)

    def used(e):
        return ((e > 0) | has_up) & ((e < nb + 1) | has_dn)

    est_load = [
        pltpu.make_async_copy(
            est.at[:, b * hw : (b + 1) * hw, :], fg.at[0, b + 1, mine(v)], lsem.at[5 + b]
        )
        for b in range(nb)
    ]
    small = [
        pltpu.make_async_copy(s, d, lsem.at[i])
        for i, (s, d) in enumerate((
            (profile_any, profile), (supports_any, supports), (scales_any, scales), (flags_any, flags),
        ))
    ]
    load = pltpu.make_async_copy(vd_any, vd, lsem.at[4])
    for c in est_load:
        c.start()
    for c in small:
        c.start()
    load.start()

    barrier = pltpu.get_barrier_semaphore()
    meets = [(None, to_a), (None, to_b), (has_up, to_up), (has_dn, to_dn)]
    for d in range(2):
        for c in range(2):
            meets.append((z_has[d], z_dev[d][c]))
            for u in range(2):
                dev = dict(z_dev[d][c], gy=y_co[u])
                meets.append((z_has[d] & y_has[u], dev))
    expected = jnp.int32(0)
    for cond, dev in meets:
        if cond is None:
            pl.semaphore_signal(barrier, inc=1, device_id=dev, device_id_type=MESH)
            expected = expected + 1
        else:
            @pl.when(cond)
            def _():
                pl.semaphore_signal(barrier, inc=1, device_id=dev, device_id_type=MESH)
            expected = expected + cond.astype(jnp.int32)

    for d in range(2):
        @pl.when(jnp.logical_not(z_has[d]))
        def _():
            for it in range(ITERS):
                for c in range(2):
                    wi[it, d, c] = jnp.zeros((ne, hw, LANES), F32)
                zi[it, d] = jnp.zeros((ne, hw, LANES), F32)

        for u, e in ((0, 0), (1, nb + 1)):
            @pl.when(z_has[d] & jnp.logical_not(y_has[u]))
            def _():
                for it in range(ITERS):
                    zi[it, d, e] = jnp.zeros((hw, LANES), F32)

    for c in est_load:
        c.wait()

    def core_send(it, e, k, group=0):
        ref = fg.at[it, e, mine(pair[k])]
        rcopy(ref, ref, sid["core"] + e, group, to_a).start()

    def y_send(it, e, ks):
        for u, e_from, e_to in ((0, 1, nb + 1), (1, nb, 0)):
            @pl.when(y_has[u] & (e == e_from))
            def _():
                for k in ks:
                    rcopy(
                        fg.at[it, e_from, mine(pair[k])], fg.at[it, e_to, mine(pair[k])],
                        sid["y"] + 1 - u, y_group(u), y_to[u],
                    ).start()

    def x_send(e):
        ref = fg.at[0, e, mine(v)]
        rcopy(ref, ref, sid["x"] + e, 0, to_b).start()

    lane_h = lane_iota(hw)
    group_h = lane_h // hw
    main = slice(1, nb + 1)

    def edge_tile(bodies):
        tile = jnp.zeros((hw, LANES), F32)
        for p, body in enumerate(bodies):
            tile = jnp.where(group_h == p, roll_lanes(body[:, :LANES], hw * p), tile)
            tile = jnp.where(
                group_h == own + p, roll_lanes(body[:, rows_z - LANES :], hw * (own + p + 1)), tile
            )
        return tile

    def edges(it, e, k):
        et[it, k, e] = edge_tile([fg[it, e, own * pair[k] + p] for p in range(own)])

    def by_side(near, far):
        return (
            jnp.where(lane_h < half, near, roll_lanes(far, half)),
            jnp.where(lane_h < half, roll_lanes(near, half), far),
        )

    def z_sid(side, e):
        return sid["z"] + side * ne + e

    def z_send(it, e):
        for d in range(2):
            for c in range(2):
                @pl.when(z_has[d])
                def _():
                    rcopy(wk.at[it, d, e], wi.at[it, 1 - d, c, e], z_sid(1 - d, e), z_group(d), z_dev[d][c]).start()

    def diag_send(it, e):
        for u, e_from, e_to in ((0, 1, nb + 1), (1, nb, 0)):
            for d in range(2):
                @pl.when(z_has[d] & y_has[u] & (e == e_from))
                def _():
                    for c in range(2):
                        rcopy(
                            wk.at[it, d, e_from], wi.at[it, 1 - d, c, e_to], z_sid(1 - d, e_to),
                            diag_group(d, u), dict(z_dev[d][c], gy=y_co[u]),
                        ).start()

    def z_split(it, e):
        wk[it, 0, e], wk[it, 1, e] = by_side(et[it, 0, e], et[it, 1, e])

    def gather(it, e):
        landed(fg.at[it, e, pl.ds(0, 2 * own)], sid["core"] + e, to_a)
        fb[pl.ds(pl.multiple_of(e * blk, blk), blk), :rows_z] = fg[it, e].reshape(blk, rows_z).astype(BF)

    def z_landed(it, e, cond_y=None):
        for side in range(2):
            cond = z_has[side] if cond_y is None else z_has[side] & cond_y
            @pl.when(cond)
            def _():
                landed(wi.at[it, side, :, e], z_sid(side, e), z_dev[side][0])

    def halo(it, e):
        for c in range(2):
            owners = pair if c == 0 else other
            pk[owners[0]], pk[owners[1]] = by_side(wi[it, 0, c, e], wi[it, 1, c, e])
        base = pl.multiple_of(e * blk, blk)
        for x in range(planes):
            rim = jnp.where(group_h % own == x % own, pk[x // own], 0.0)
            fb[pl.ds(base + x * hw, hw), rows_z:] = rim.astype(BF)

    def rim_forward(it):
        for u, e in ((0, 0), (1, nb + 1)):
            @pl.when(y_has[u])
            def _():
                landed(fg.at[it, e, pl.ds(0, 2 * own)], sid["y"] + u, y_to[u])
                for k in range(2):
                    core_send(it, e, k, y_group(u))

    def rim_gather(it, e):
        @pl.when(used(e))
        def _():
            gather(it, e)
            z_landed(it, e, used(e))
            halo(it, e)

    def forward(e):
        b = e - 1
        base = pl.multiple_of(b * blk, blk)
        g = jnp.dot(am[...], fb[pl.ds(base, 3 * blk), :], preferred_element_type=F32).astype(BF)
        z_block = lax.broadcasted_iota(jnp.int32, (1, rows_z), 1) // BZ
        y_block = b * hw // BY
        for vv in range(views):
            scale = jnp.zeros((1, rows_z), F32)
            valid = jnp.zeros((1, rows_z), jnp.int32)
            for c in range(rows_z // BZ):
                scale = jnp.where(z_block == c, scales[vv, y_block, c], scale)
                valid = jnp.where(z_block == c, flags[vv, y_block, c], valid)
            blurred = lax.dot_general(
                g[vv * blk : (vv + 1) * blk], mt[vv], (((1,), (1,)), ((), ())),
                preferred_element_type=F32,
            )
            data = vd[vv, :, pl.ds(pl.multiple_of(b * hw, hw), hw), :].astype(F32)
            ratio = jnp.where(
                valid == 1, data.reshape(blk, rows_z) * (scale * gains[vv][0]) / blurred, 1.0
            )
            spread = jnp.dot((ratio * gains[vv][1]).astype(BF), mt[vv], preferred_element_type=F32)
            spread = spread.astype(BF)
            gp[vv, pl.ds(base + 2 * blk, blk), :] = spread[:, :rows_z]
            gh[vv, pl.ds(base + 2 * blk, blk), :LANES] = spread[:, rows_z:]
            gh[vv, pl.ds(base + blk, blk), LANES:] = spread[:, rows_z:]

    def r1_send(it, e, group=0):
        for k in range(2):
            rcopy(ob.at[it, e, mine(other[k])], r1.at[it, e, k], sid["r1"] + e, group, to_a).start()

    def back(it, e, rim=False):
        if rim:
            rows = pl.ds(pl.multiple_of(jnp.where(e == 0, 2, nb + 1) * blk, blk), blk)
            taken = pl.ds(pl.multiple_of(jnp.where(e == 0, 2, 0) * blk, blk), blk)
        else:
            rows = pl.ds(pl.multiple_of(e * blk, blk), 3 * blk)
            taken = slice(None)
        total = jnp.dot(bm[0, :, taken], gp[0, rows, :], preferred_element_type=F32)
        for vv in range(1, views):
            total = total + jnp.dot(bm[vv, :, taken], gp[vv, rows, :], preferred_element_type=F32)
        ob[it, e] = total.reshape(planes, hw, rows_z)
        if not rim:
            r1_send(it, e)
        else:
            for u, e_rim in ((0, 0), (1, nb + 1)):
                @pl.when(e == e_rim)
                def _():
                    r1_send(it, e_rim, y_group(u))

    def z_pair(it, e):
        lo, hi = (1 if e == 0 else 0, 2 if e + 2 == ne else 3)
        rows = slice((e + lo) * blk, (e + hi) * blk)
        taken = slice(lo * blk, hi * blk)
        total = jnp.dot(bm[0, :, taken], gh[0, rows, :], preferred_element_type=F32)
        for vv in range(1, views):
            total = total + jnp.dot(bm[vv, :, taken], gh[vv, rows, :], preferred_element_type=F32)
        rims = total.reshape(planes, hw, 2 * LANES)
        for n in range(2):
            for o in range(planes // own):
                packed = rims[own * o, :, n * LANES : (n + 1) * LANES]
                for p in range(1, own):
                    rim = rims[own * o + p, :, n * LANES : (n + 1) * LANES]
                    packed = jnp.where(group_h % own == p, rim, packed)
                zp[it, o, e + n] = packed

    def z_rims_sum(it):
        for k in range(2):
            rcopy(zp.at[it, other[k]], r1z.at[it, k], sid["r1z"], 0, to_a).start()

    zb_kinds = (
        (slice(1, nb + 1), None, slice(1, nb + 1)),
        (slice(0, 1), 0, slice(nb + 1, nb + 2)),
        (slice(nb + 1, nb + 2), 1, slice(0, 1)),
    )

    def each_zb(fn, landing=False):
        for d in range(2):
            for n, (src, u, dst) in enumerate(zb_kinds):
                u = 1 - u if landing and u is not None else u
                cond = z_has[d] if u is None else z_has[d] & y_has[u]
                dev = z_dev[d][0] if u is None else dict(z_dev[d][0], gy=y_co[u])
                @pl.when(cond)
                def _():
                    fn(d, n, src, dst, z_group(d) if u is None else diag_group(d, u), dev)

    def z_rims_send(it):
        landed(r1z.at[it], sid["r1z"], to_a)
        for e in range(ne):
            zo[it, 0, e], zo[it, 1, e] = by_side(
                zp[it, v, e] + r1z[it, 0, e], zp[it, vb, e] + r1z[it, 1, e]
            )
        each_zb(lambda d, n, src, dst, group, dev: rcopy(
            zo.at[it, d, src], zi.at[it, 1 - d, dst], sid["zb"] + 3 * (1 - d) + n, group, dev
        ).start())

    def z_rims_take(it, order, raw):
        each_zb(lambda d, n, src, dst, group, dev: landed(
            zi.at[it, d, dst], sid["zb"] + 3 * d + n, dev), True)
        for e in range(1, nb + 1):
            lf, rt = (zi[it, 0, e], zi[it, 1, e])
            if e == 1:
                lf, rt = (lf + zi[it, 0, 0], rt + zi[it, 1, 0])
            if e == nb:
                lf, rt = (lf + zi[it, 0, nb + 1], rt + zi[it, 1, nb + 1])
            zt[it, 0, e], zt[it, 1, e] = by_side(lf, rt)
        last = it + 1 == ITERS
        for n in range(raw):
            zx[it, 0, n] = zt[it, 1, order[n]]
            zx[it, 1, n] = zt[it, 0, order[n]]
        for k in range(1 if last else 2):
            rcopy(zx.at[it, k, :raw], zr.at[it, k, :raw], sid["zx"] + it, 0, to_b).start()

    def side_parts(tile, p):
        first = roll_lanes(tile, -hw * p)
        final = roll_lanes(tile, LANES - hw - half - hw * p)
        return jnp.where(lane_h < hw, first, 0.0), jnp.where(lane_h >= LANES - hw, final, 0.0)

    def rim_finish(it, e):
        landed(r1.at[it, e], sid["r1"] + e, to_a)
        for k in range(2):
            tt[it, e, k] = ob[it, e, mine(pair[k])] + r1[it, e, k]
        for u, e_from in ((0, 0), (1, nb + 1)):
            @pl.when(y_has[u] & (e == e_from))
            def _():
                rcopy(tt.at[it, e_from], yi.at[it, 1 - u], sid["yb"] + 1 - u, y_group(u), y_to[u]).start()

    def finish(it, e, edge, with_rims, send=True):
        landed(r1.at[it, e], sid["r1"] + e, to_a)
        if edge:
            for u, e_to in ((0, 1), (1, nb)):
                @pl.when(y_has[u] & (e == e_to))
                def _():
                    landed(yi.at[it, u], sid["yb"] + u, y_to[u])
        for k in (1, 0):
            tt[it, e, k] = ob[it, e, mine(pair[k])] + r1[it, e, k]
            if edge:
                for u, e_to in ((0, 1), (1, nb)):
                    @pl.when(y_has[u] & (e == e_to))
                    def _():
                        tt[it, e, k] = tt[it, e, k] + yi[it, u, k]
            if with_rims:
                for p in range(own):
                    first, final = side_parts(zt[it, k, e], p)
                    tt[it, e, k, p, :, :LANES] += first
                    tt[it, e, k, p, :, rows_z - LANES :] += final
        if send:
            sums_send(it, e)

    def sums_send(it, e):
        last = it + 1 == ITERS
        for k in (1,) if last else (1, 0):
            rcopy(tt.at[it, e, k], r2.at[it, e, 1 - k], sid["r2"] + it * ne + e, 0, to_b).start()

    def rest_send(it, order, raw):
        count = nb - raw
        for k in range(2):
            for n in range(count):
                te[it, 1 - k, n] = edge_tile([tt[it, order[raw + n], k, p] for p in range(own)])
        rcopy(te.at[it, :, :count], re.at[it, :, :count], sid["te"], 0, to_b).start()
        for n in range(raw, nb):
            sums_send(it, order[n])

    def rest_edges(it, order, raw):
        landed(re.at[it - 1, :, : nb - raw], sid["te"], to_b)
        for n in range(raw, nb):
            e = order[n]
            for k in range(2):
                total = te[it - 1, 1 - k, n - raw] + re[it - 1, k, n - raw]
                et[it, k, e] = et[it - 1, k, e] * total / view_total
            z_split(it, e)
            z_send(it, e)
            diag_send(it, e)

    def corrected(it, e, k, n, raw):
        tile = zt[it, k, e] + zr[it, k, n] if n < raw else None
        for p in range(own):
            total = tt[it, e, k, p] + r2[it, e, k, p]
            if tile is not None:
                first, final = side_parts(tile, p)
                total = jnp.concatenate([
                    total[:, :LANES] + first, total[:, LANES : rows_z - LANES],
                    total[:, rows_z - LANES :] + final,
                ], axis=1) if rows_z > 2 * LANES else jnp.concatenate(
                    [total[:, :LANES] + first, total[:, LANES:] + final], axis=1)
            yield p, fg[it, e, own * pair[k] + p] * total / view_total

    def m(e):
        return flipped(e)

    for e in range(1, nb + 1):
        edges(0, e, 0)
    with scope("barrier"):
        pl.semaphore_wait(barrier, expected)

    load_order = [m(e) for e in range(nb, 0, -1)]
    rcopy(et.at[0, 0, main], et.at[0, 1, main], sid["x"], 0, to_b).start()
    x_send(load_order[0])
    core_send(0, load_order[0], 0)
    y_send(0, m(nb), (0,))
    y_send(0, m(1), (0,))
    for e in load_order[1:]:
        x_send(e)
        core_send(0, e, 0)

    with scope("build"):
        for c in small:
            c.wait()
        build_taps(taps, profile, supports, views)
        for vv in range(views):
            build_depth(mt, vv, taps[0, 3 * vv + 2 : 3 * vv + 3, :], rows_z, hw)
            build_plane_row(
                am, vv * blk, taps[0, 3 * vv : 3 * vv + 1, :],
                taps[0, 3 * vv + 1 : 3 * vv + 2, :], planes, hw,
            )
        for e in (0, nb + 1):
            fb[e * blk : (e + 1) * blk, :] = jnp.zeros((blk, rows_z + LANES), BF)
    gains = []

    def build_backward():
        for vv in range(views):
            build_plane_row(
                bm.at[vv], 0, taps[1, 3 * vv : 3 * vv + 1, :],
                taps[1, 3 * vv + 1 : 3 * vv + 2, :], planes, hw,
            )
            for e in (0, 1, nb + 2, nb + 3):
                gp[vv, e * blk : (e + 1) * blk, :] = jnp.zeros((blk, rows_z), BF)
                gh[vv, e * blk : (e + 1) * blk, :LANES] = jnp.zeros((blk, LANES), BF)
            for e in (-1, 0, nb + 1, nb + 2, nb + 3):
                if e >= 0:
                    gh[vv, e * blk : (e + 1) * blk, LANES:] = jnp.zeros((blk, LANES), BF)
        for vv in range(views):
            mid = planes // 2 * hw
            along_z = mt[vv, rows_z // 2 : rows_z // 2 + 1, :rows_z].astype(F32)
            along_z = jnp.sum(along_z, axis=1, keepdims=True)
            fwd = am[vv * blk + mid : vv * blk + mid + 1, :].astype(F32)
            bwd = bm[vv, mid : mid + 1, :].astype(F32)
            gains.append((
                jnp.sum(fwd, axis=1, keepdims=True) * along_z,
                1.0 / (jnp.sum(bwd, axis=1, keepdims=True) * along_z),
            ))

    def raw_of(it):
        return nb if it + 1 == ITERS else 2

    def load_first(e):
        landed(fg.at[0, e, mine(vb)], sid["x"] + e, to_b)
        core_send(0, e, 1)

    def step_order(it):
        mid_order = [m(nb - 1), m(nb)] + [m(e) for e in range(nb - 2, 0, -1)]
        last_order = [m(e) for e in range(nb - 1, 0, -1)] + [m(nb)]
        return last_order if it + 1 == ITERS else mid_order

    def prepare_first(i):
        if i == 0:
            with scope('p_et'):
                landed(et.at[0, 1, main], sid["x"], to_b)
            for e in range(1, nb + 1):
                z_split(0, e)
            for d in range(2):
                for c in range(2):
                    @pl.when(z_has[d])
                    def _():
                        rcopy(
                            wk.at[0, d, main], wi.at[0, 1 - d, c, main], z_sid(1 - d, 1), z_group(d), z_dev[d][c]
                        ).start()
            diag_send(0, 1)
            diag_send(0, nb)
            with scope('p_first'):
                load_first(load_order[0])
            y_send(0, load_order[0], (1,))
            with scope("p_bb"):
                build_backward()
            for n, e in enumerate(load_order[1:-1]):
                with scope("p_x"):
                    load_first(e)
                if n < nb - 3:
                    gather(0, load_order[n])
            with scope("p_z"):
                for side in range(2):
                    @pl.when(z_has[side])
                    def _():
                        landed(wi.at[0, side, :, main], z_sid(side, 1), z_dev[side][0])
                for q in load_order:
                    halo(0, q)
            gather(0, load_order[-3])
            with scope("p_rimf"):
                rim_forward(0)
            load.wait()
            with scope("p_gather"):
                gather(0, load_order[-2])
        elif i == 1:
            load_first(load_order[-1])
            y_send(0, load_order[-1], (1,))
            rim_gather(0, m(nb + 1))
        elif i == 2:
            gather(0, load_order[-1])
        elif i == 3:
            rim_gather(0, m(0))

    def update(it, n):
        order = step_order(it - 1)
        e = order[n]
        raw = raw_of(it - 1)
        if n == 0:
            landed(zr.at[it - 1, :, :raw], sid["zx"] + it - 1, to_b)
        landed(r2.at[it - 1, e], sid["r2"] + (it - 1) * ne + e, to_b)
        for k in range(2):
            for p, fresh in corrected(it - 1, e, k, n, raw):
                fg[it, e, own * pair[k] + p] = fresh
            core_send(it, e, k)
            if n < raw:
                edges(it, e, k)
        y_send(it, e, (0, 1))
        if n < raw:
            z_split(it, e)
            z_send(it, e)
            diag_send(it, e)

    def sends_done():
        plane, tile = rows_z // LANES, 1
        block = 2 * own * plane
        total = [0] * 9
        for it in range(ITERS):
            last = it + 1 == ITERS
            raw = raw_of(it)
            total[0] += nb * block * 2 + 2 * ne + nb * block // (2 if last else 1)
            total[0] += raw if last else 2 * nb
            total[0] += nb * block // 2 + nb if it == 0 else 0
            for u in range(2):
                total[y_group(u)] += 4 * block
            for d in range(2):
                total[z_group(d)] += 2 * nb + nb
                for u in range(2):
                    total[diag_group(d, u)] += 3
        conds = [None, *y_has, *z_has, *(z_has[d] & y_has[u] for d in range(2) for u in range(2))]
        for group, (tiles, cond) in enumerate(zip(total, conds)):
            def done():
                ref = count.at[pl.ds(0, tiles)]
                rcopy(ref, ref, 0, group, to_a).wait_send()
            if cond is None:
                done()
            else:
                pl.when(cond)(done)

    def prepare_next(it, i):
        order = step_order(it - 1)
        if i == 0:
            raw = raw_of(it - 1)
            for n in range(nb - 1):
                with scope(f"upd{n}"):
                    update(it, n)
                if n == raw - 1:
                    with scope("rest"):
                        rest_edges(it, order, raw)
                    for q in range(n):
                        gather(it, order[q])
                        z_landed(it, order[q])
                        halo(it, order[q])
            with scope("gath"):
                for q in range(raw - 1, nb - 1):
                    z_landed(it, order[q])
                    halo(it, order[q])
                    gather(it, order[q])
                z_landed(it, order[nb - 1])
                halo(it, order[nb - 1])
        elif i == 1:
            with scope("rimf"):
                rim_forward(it)
            with scope("upd3"):
                update(it, nb - 1)
            with scope("rimg"):
                rim_gather(it, m(nb + 1))
        elif i == 2:
            with scope("gath"):
                gather(it, order[nb - 1])
        elif i == 3:
            rim_gather(it, m(0))

    def out_copy(n, e):
        rows = pl.ds(pl.multiple_of((e - 1) * hw, hw), hw)
        return pltpu.make_async_copy(ov.at[e], out.at[:, rows, :], lsem.at[5 + n])

    for it in range(ITERS):
        last = it + 1 == ITERS
        order = step_order(it)
        raw = raw_of(it)
        top = (nb - 1, nb)
        rim = m(nb + 1)
        far = m(0)
        near = jnp.where(has_dn, nb, 0)
        with scope(f"prep{it}0"):
            prepare_first(0) if it == 0 else prepare_next(it, 0)

        @pl.loop(0, nb)
        def _(i):
            for n in range(1, 4):
                @pl.when(i == n)
                def _():
                    with scope(f"prep{it}{n}"):
                        prepare_first(n) if it == 0 else prepare_next(it, n)
            e = jnp.where(i == 0, top[0], jnp.where(i == 1, top[1], nb - i))
            with scope(f"fwd{it}"):
                forward(m(e))

            @pl.when((e == nb) & used(rim))
            def _():
                with scope(f"rimb{it}"):
                    back(it, rim, True)

            @pl.when((i == 2) & used(rim))
            def _():
                with scope(f"rimfin{it}"):
                    rim_finish(it, rim)

            @pl.when(i == 2)
            def _():
                with scope(f"back{it}"):
                    back(it, order[0])

        with scope(f"tail{it}"):
            @pl.when(used(far))
            def _():
                back(it, far, True)
            with scope(f"fin{it}"):
                finish(it, order[0], False, False)
            if last:
                back(it, order[1])
            with scope(f"zrim{it}"):
                for e in range(0, ne, 2):
                    z_pair(it, e)
            z_rims_sum(it)
            if not last:
                back(it, order[1])

            @pl.when(used(far))
            def _():
                rim_finish(it, far)
            back(it, order[2])
            if last:
                with scope(f"fin{it}"):
                    finish(it, order[1], False, False)
            with scope(f"zrs{it}"):
                z_rims_send(it)
            if not last:
                with scope(f"fin{it}"):
                    finish(it, order[1], True, False)
            for n in range(3, nb):
                back(it, order[n])
            if last:
                for n in range(2, nb):
                    with scope(f"fin{it}"):
                        finish(it, order[n], n >= nb - 2, False)
                with scope(f"zrt{it}"):
                    z_rims_take(it, order, raw)
            else:
                with scope(f"zrt{it}"):
                    z_rims_take(it, order, raw)
                for n in range(2, nb):
                    with scope(f"fin{it}"):
                        finish(it, order[n], n == nb - 1, True, False)
                with scope(f"rests{it}"):
                    rest_send(it, order, raw)

        if last:
            for n in range(nb):
                with scope("final"):
                    e = order[n]
                    if n == 0:
                        landed(zr.at[it, 0, :raw], sid["zx"] + it, to_b)
                    landed(r2.at[it, e, 0], sid["r2"] + it * ne + e, to_b)
                    for p, fresh in corrected(it, e, 0, n, raw):
                        ov[e, p] = fresh
                    out_copy(n, e).start()
            for n in range(nb):
                out_copy(n, order[n]).wait()
            with scope("sentx"):
                sends_done()


def per_device(ny, nz, estimate, view_data, block_scales, block_flags, profile, supports):
    views, planes, rows_y, rows_z = view_data.shape
    own = estimate.shape[0]
    hw = (profile.shape[2] - 1) // 2
    nb = rows_y // hw
    ne = nb + 2
    blk = planes * hw
    wide = rows_z + LANES
    tap_rows = -(-3 * views // 8) * 8
    owners = planes // own
    _, n_sem = sem_bases(ne)
    n = ITERS
    vm = pltpu.VMEM
    table = jnp.transpose(profile, (1, 0, 2))
    scratch = [
        pltpu.SMEM(block_scales.shape, F32),
        pltpu.SMEM(block_flags.shape, jnp.int32),
        vm(table.shape, F32),
        pltpu.SMEM(supports.shape, jnp.int32),
        vm((2, tap_rows, LANES), F32),
        vm((n, ne, planes, hw, rows_z), F32),
        vm((ne * blk, wide), BF),
        vm((views * blk, 3 * blk), BF),
        vm((views, blk, 3 * blk), BF),
        vm((views, rows_z, wide), BF),
        vm((views, (nb + 4) * blk, rows_z), BF),
        vm((views, (nb + 4) * blk, 2 * LANES), BF),
        vm((n, ne, planes, hw, rows_z), F32),
        vm((n, ne, 2, own, hw, rows_z), F32),
        vm((n, ne, 2, own, hw, rows_z), F32),
        vm((n, ne, 2, own, hw, rows_z), F32),
        vm((n, 2, 2, own, hw, rows_z), F32),
        vm((n, 2, ne, hw, LANES), F32),
        vm((n, 2, ne, hw, LANES), F32),
        vm((n, 2, 2, ne, hw, LANES), F32),
        vm((owners, hw, LANES), F32),
        vm((n, owners, ne, hw, LANES), F32),
        vm((n, 2, ne, hw, LANES), F32),
        vm((n, 2, ne, hw, LANES), F32),
        vm((n, 2, ne, hw, LANES), F32),
        vm((n, 2, ne, hw, LANES), F32),
        vm((n, 2, nb, hw, LANES), F32),
        vm((n, 2, nb, hw, LANES), F32),
        vm((n, 2, nb, hw, LANES), F32),
        vm((n, 2, nb, hw, LANES), F32),
        vm(view_data.shape, view_data.dtype),
        vm((2 * n * ne * planes * rows_z // LANES, hw, LANES), F32),
        vm((ne, own, hw, rows_z), F32),
        pltpu.SemaphoreType.DMA((5 + nb,)),
        pltpu.SemaphoreType.DMA((9,)),
        pltpu.SemaphoreType.DMA((n_sem,)),
    ]
    in_hbm = pl.BlockSpec(memory_space=pltpu.HBM)
    return pl.pallas_call(
        functools.partial(kernel, (ny, nz, views, planes, rows_y, rows_z, own, hw)),
        out_shape=jax.ShapeDtypeStruct(estimate.shape, F32),
        in_specs=[in_hbm] * 6,
        out_specs=pl.BlockSpec(memory_space=pl.ANY),
        scratch_shapes=scratch,
        compiler_params=pltpu.CompilerParams(
            collective_id=0, has_side_effects=True, vmem_limit_bytes=48 * 1024 * 1024
        ),
    )(*(
        pltpu.with_memory_space_constraint(x, pltpu.HBM)
        for x in (estimate, view_data, block_scales, block_flags, table, supports)
    ))


def solution(mesh):
    placed = (
        P("view", "gy", "gz"),
        P("view", None, "gy", "gz"),
        P("view", "gy", "gz"),
        P("view", "gy", "gz"),
        P("view", None, None),
        P("view", None),
    )
    body = functools.partial(per_device, mesh.shape["gy"], mesh.shape["gz"])
    return jax.shard_map(
        body, mesh=mesh, in_specs=placed, out_specs=P("view", "gy", "gz"), check_vma=False
    )
```
